32 devices in a mesh: dp: 16 (over z, x, core), tensor: 2 (over y).
Axes of the slice: x: 2, y: 2, z: 4, core: 2. Of those that a mesh axis runs over, the one named last changes fastest.
Arguments:
- tokens: bfloat16 [512, 3584], P(('dp', 'tensor')), may hold values from -6 to 6
- cotangent: bfloat16 [512, 3584], P(('dp', 'tensor')), may hold values from -3 to 3
- gates: bfloat16 [512, 8], P(('dp', 'tensor')), may hold values from 0.049804688 to 0.59765625
- routes: int32 [512, 8], P(('dp', 'tensor')), may hold values from 0 to 15, all different within a row; in each aligned block of 16 rows (0 to 15, 16 to 31, ...) at most 9 rows name the same one
- gate_weight: bfloat16 [16, 3584, 1024], P('dp', None, 'tensor'), may hold values from -0.09375 to 0.09375
- up_weight: bfloat16 [16, 3584, 1024], P('dp', None, 'tensor'), may hold values from -0.09375 to 0.09375
- down_weight: bfloat16 [16, 1024, 3584], P('dp', 'tensor'), may hold values from -0.1875 to 0.1875
Outputs:
- input_grad: bfloat16 [512, 3584], P(('dp', 'tensor'))
- gate_grad: bfloat16 [16, 3584, 1024], P('dp', None, 'tensor')
- up_grad: bfloat16 [16, 3584, 1024], P('dp', None, 'tensor')
- down_grad: bfloat16 [16, 1024, 3584], P('dp', 'tensor')
The draws below stay inside these ranges and needn't reach their ends.
Inputs may be any that keep to these rules, and one draw needn't show every extreme that they name: `routes`: A token names 8 different experts; among the 16 tokens of one device no expert is named by more than 9 tokens, a bound that some block reaches.
All inputs are finite; a program needn't handle non-finite values.
Results may differ from the reference program's by a relative error of at most 0.0085.
Values may be sent and summed in bfloat16 or wider, within the bound.
A program may use at most 128 MiB of HBM per device.

```python
import math
import jax
import jax.numpy as jnp
import numpy as np
from jax import lax

D = 3584
FF = 1024
TOP = 8
TOK_DEV = 16
EXPERTS = 16
CAP = 9
TOKENS = 512
N_TENSOR = 2


def steps_of(rng, shape, shards, low, largest):
    level = 1.0
    for dim, blocks in shards:
        steps = jax.random.uniform(jax.random.fold_in(jax.random.fold_in(rng, 6), dim), (blocks,), jnp.float32, low / len(shards), largest / len(shards))
        level = level * jnp.repeat(jnp.exp(steps), shape[dim] // blocks).reshape((-1,) + (1,) * (len(shape) - 1 - dim))
    return level


def shared_out(stream_key, own, number, rows, amount, top, limit, lean):
    order = jax.random.permutation(stream_key, amount)
    packed, ordinary = portions_of(amount, rows * top, limit, lean, True), portions_of(amount, rows * top, limit, lean, False)
    places = jnp.arange(amount)

    def named(sizes, offset_by):
        used = int((sizes > 0).sum())
        fixed = max(1, used // 4)
        passed = fixed + (places - fixed + offset_by * (used - fixed)) % max(1, amount - fixed)
        return jnp.zeros((amount,), jnp.int32).at[order[jnp.where(places < fixed, places, passed)]].set(jnp.asarray(sizes, jnp.int32))

    sizes = jnp.where(number % 4 == 0, named(packed, number // 4), named(ordinary, number - number // 4 - 1))
    mixed = jax.random.permutation(jax.random.fold_in(own, 3), amount)
    source_of, taker = mixed[0:amount // 2 * 2:2], mixed[1:amount // 2 * 2:2]
    margin = jnp.minimum(sizes[source_of] - 1, limit - sizes[taker]) // 2
    margin = jnp.where((source_of == order[0]) | (taker == order[0]) | (sizes[taker] == 0), 0, jnp.maximum(margin, 0))
    passed = jax.random.randint(jax.random.fold_in(own, 4), (amount // 2,), 0, 1 << 20) % (margin + 1)
    sizes = sizes.at[source_of].add(-passed).at[taker].add(passed)
    items = jnp.searchsorted(jnp.cumsum(sizes), jnp.arange(rows * top), side="right").astype(jnp.int32)
    grid = items.reshape(top, rows).T
    grid = grid[jax.random.permutation(jax.random.fold_in(own, 1), rows)]
    offset_by = jax.random.randint(jax.random.fold_in(own, 2), (rows, 1), 0, top)
    return jnp.take_along_axis(grid, (jnp.arange(top)[None, :] + offset_by) % top, axis=1)


def portions_of(count, total, most, skew, full):
    weights = [(1 << 20) // math.isqrt(grade ** skew) + 1 for grade in range(1, count + 1)]
    largest = most if full else min(most, max(-(-total // count), total * weights[0] // sum(weights)))
    least = 1 if total - largest >= count - 1 else 0
    counts, rest = [largest] + [least] * (count - 1), total - largest - least * (count - 1)
    while rest > 0:
        candidates = [i for i in range(1, count) if counts[i] < largest] or [i for i in range(1, count) if counts[i] < most]
        mass, budget = sum([weights[i] for i in candidates]), rest
        for i in candidates:
            extra = min(most - counts[i], max(1, budget * weights[i] // mass), rest)
            counts[i] = counts[i] + extra
            rest = rest - extra
    return np.array(counts)


def noise(key, dims, width, bound, split=(), kind=jnp.bfloat16):
    gain = steps_of(key, dims, split, -0.22, 0.18) if split else 1.0
    array = jax.random.normal(key, dims, jnp.float32) * width * gain
    return jnp.minimum(jnp.maximum(array, -bound), bound).astype(kind)


def setup_inputs(seed: int = 0) -> dict:
    key_list = jax.random.split(jax.random.key(seed), 8)
    tokens = noise(key_list[0], (TOKENS, D), 1.0, 6.0, ((0, 32),))
    cotangent = noise(key_list[1], (TOKENS, D), 0.5, 3.0, ((0, 32),))
    gates = jnp.clip(jnp.exp(math.log(0.59765625) - 2.4849066 * jax.random.uniform(key_list[2], (TOKENS, TOP), jnp.float32) ** steps_of(key_list[2], (TOKENS, TOP), ((0, 32),), -0.2, 0.2)), 0.049804688, 0.59765625).astype(jnp.bfloat16)
    routes_keys = jax.random.split(jax.random.fold_in(key_list[3], 1), TOKENS // TOK_DEV)
    routes_turns = jax.random.permutation(jax.random.fold_in(key_list[3], 3), TOKENS // TOK_DEV)
    routes = jax.vmap(lambda own, number: shared_out(jax.random.fold_in(key_list[3], 2), own, number, TOK_DEV, EXPERTS, TOP, CAP, 2))(routes_keys, routes_turns).reshape((TOKENS, TOP))
    gate_weight = noise(key_list[4], (EXPERTS, D, FF), D ** -0.5, 0.09375, ((0, 16), (2, 2)))
    up_weight = noise(key_list[5], (EXPERTS, D, FF), D ** -0.5, 0.09375, ((0, 16), (2, 2)))
    down_weight = noise(key_list[6], (EXPERTS, FF, D), FF ** -0.5, 0.1875, ((0, 16), (1, 2)))
    return {"tokens": tokens, "cotangent": cotangent, "gates": gates, "routes": routes, "gate_weight": gate_weight, "up_weight": up_weight, "down_weight": down_weight}


def contract(left, right, left_dim, right_dim):
    return lax.dot_general(left, right, (((left_dim,), (right_dim,)), ((), ())), preferred_element_type=jnp.float32)


def reference(tokens, cotangent, gates, routes, gate_weight, up_weight, down_weight):
    max_rows = (TOKENS // TOK_DEV) * CAP
    hidden_dev = FF // N_TENSOR
    gate_values = gates.astype(jnp.float32)
    positions = jnp.arange(max_rows)

    def expert_pass(dx_total, inputs):
        w_gate, w_up, w_down, expert = inputs
        hit = routes == expert
        weight_token = jnp.sum(jnp.where(hit, gate_values, jnp.float32(0.0)), axis=1)
        used = jnp.any(hit, axis=1)
        picked = jnp.nonzero(used, size=max_rows, fill_value=0)[0]
        valid = (positions < jnp.sum(used)).astype(jnp.float32)
        x_rows = tokens[picked]
        dy_rows = (cotangent[picked].astype(jnp.float32) * valid[:, None]).astype(jnp.bfloat16)
        scale_rows = weight_token[picked] * valid
        gate_pre = jnp.dot(x_rows, w_gate, preferred_element_type=jnp.float32)
        up_pre = jnp.dot(x_rows, w_up, preferred_element_type=jnp.float32)
        sig = jax.nn.sigmoid(gate_pre)
        act = gate_pre * sig
        hidden = (act * up_pre).astype(jnp.bfloat16)
        d_hidden = scale_rows[:, None] * contract(dy_rows, w_down, 1, 1)
        d_up = (d_hidden * act).astype(jnp.bfloat16)
        d_gate = (d_hidden * up_pre * sig * (1.0 + gate_pre * (1.0 - sig))).astype(jnp.bfloat16)
        grad_down = contract(hidden, dy_rows, 0, 0).astype(jnp.bfloat16)
        grad_gate = contract(x_rows, d_gate, 0, 0).astype(jnp.bfloat16)
        grad_up = contract(x_rows, d_up, 0, 0).astype(jnp.bfloat16)
        dg_split = d_gate.astype(jnp.float32).reshape(max_rows, N_TENSOR, hidden_dev)
        du_split = d_up.astype(jnp.float32).reshape(max_rows, N_TENSOR, hidden_dev)
        wg_split = w_gate.astype(jnp.float32).reshape(D, N_TENSOR, hidden_dev)
        wu_split = w_up.astype(jnp.float32).reshape(D, N_TENSOR, hidden_dev)
        parts = jnp.einsum("rtf,dtf->trd", dg_split, wg_split) + jnp.einsum("rtf,dtf->trd", du_split, wu_split)
        parts_low = lax.optimization_barrier(parts.astype(jnp.bfloat16))
        slot_dx = jnp.sum(parts_low.astype(jnp.float32), axis=0).astype(jnp.bfloat16)
        dx_total = dx_total.at[picked].add(slot_dx.astype(jnp.float32) * valid[:, None])
        return dx_total, (grad_gate, grad_up, grad_down)

    expert_ids = jnp.arange(EXPERTS).astype(jnp.int32)
    start_total = jnp.zeros((TOKENS, D), jnp.float32)
    dx_total, grads = lax.scan(expert_pass, start_total, (gate_weight, up_weight, down_weight, expert_ids))
    return dx_total.astype(jnp.bfloat16), grads[0], grads[1], grads[2]
```

```python
import jax
import jax.numpy as jnp
from jax import lax
from jax.experimental import pallas as pl
from jax.experimental.pallas import tpu as pltpu
from jax.sharding import PartitionSpec as P


def contract(left, right, left_dim, right_dim):
    return lax.dot_general(
        left, right, (((left_dim,), (right_dim,)), ((), ())), preferred_element_type=jnp.float32
    )


def per_device_routed(tokens, cotangent, gates, routes, gate_weight, up_weight, down_weight):
    dp_count = lax.axis_size("dp")
    tok_rows = tokens.shape[0]
    model_width = tokens.shape[1]
    top_count = routes.shape[1]
    capacity = min(tok_rows, tok_rows * top_count // dp_count + 1)
    w_gate = gate_weight[0]
    w_up = up_weight[0]
    w_down = down_weight[0]
    flat_routes = routes.reshape(-1)
    expert_ids = jnp.arange(dp_count, dtype=jnp.int32)
    route_table = (flat_routes[:, None] == expert_ids[None, :]).astype(jnp.int32)
    pair_ids = jnp.arange(flat_routes.shape[0], dtype=jnp.int32)
    earlier = (pair_ids[None, :] < pair_ids[:, None]).astype(jnp.bfloat16)
    route_rank = jnp.dot(
        earlier, route_table.astype(jnp.bfloat16), preferred_element_type=jnp.float32
    ).astype(jnp.int32)
    slot_index = jnp.sum(route_table * (expert_ids[None, :] * capacity + route_rank), axis=1)
    slot_ids = jnp.arange(dp_count * capacity, dtype=jnp.int32)
    picked = slot_index[None, :] == slot_ids[:, None]
    picked_tok = jnp.any(picked.reshape(dp_count * capacity, tok_rows, top_count), axis=2).astype(
        jnp.bfloat16
    )
    x_send = jnp.dot(picked_tok, tokens, preferred_element_type=jnp.float32).astype(jnp.bfloat16)
    dy_send = jnp.dot(picked_tok, cotangent, preferred_element_type=jnp.float32).astype(
        jnp.bfloat16
    )
    p_send = jnp.sum(
        jnp.where(picked, gates.reshape(-1)[None, :].astype(jnp.float32), jnp.float32(0.0)), axis=1
    )
    x_send = x_send.reshape(dp_count, 1, capacity, model_width)
    dy_send = dy_send.reshape(dp_count, 1, capacity, model_width)
    p_send = p_send.astype(jnp.bfloat16).reshape(dp_count, 1, capacity)
    grouped = (
        lax.all_gather(x_send, "tensor", axis=1, tiled=True),
        lax.all_gather(dy_send, "tensor", axis=1, tiled=True),
        lax.all_gather(p_send, "tensor", axis=1, tiled=True),
    )
    x_block = lax.all_to_all(grouped[0], "dp", split_axis=0, concat_axis=0, tiled=True)
    dy_block = lax.all_to_all(grouped[1], "dp", split_axis=0, concat_axis=0, tiled=True)
    p_block = lax.all_to_all(grouped[2], "dp", split_axis=0, concat_axis=0, tiled=True)
    lead_shape = x_block.shape[:3]
    x_rows = x_block.reshape(-1, model_width)
    dy_rows = dy_block.reshape(-1, model_width)
    scale_rows = p_block.reshape(-1).astype(jnp.float32)
    gate_pre = jnp.dot(x_rows, w_gate, preferred_element_type=jnp.float32)
    up_pre = jnp.dot(x_rows, w_up, preferred_element_type=jnp.float32)
    sig = jax.nn.sigmoid(gate_pre)
    act = gate_pre * sig
    hidden = (act * up_pre).astype(jnp.bfloat16)
    d_hidden = scale_rows[:, None] * contract(dy_rows, w_down, 1, 1)
    d_up = (d_hidden * act).astype(jnp.bfloat16)
    d_gate = (d_hidden * up_pre * sig * (1.0 + gate_pre * (1.0 - sig))).astype(jnp.bfloat16)
    grad_down = contract(hidden, dy_rows, 0, 0)
    grad_gate = contract(x_rows, d_gate, 0, 0)
    grad_up = contract(x_rows, d_up, 0, 0)
    dx_rows = contract(d_gate, w_gate, 1, 1) + contract(d_up, w_up, 1, 1)
    dx_rows = dx_rows.reshape(lead_shape + (model_width,))
    dx_part = dx_rows
    totals = (grad_gate, grad_up, grad_down, dx_part)
    grad_gate, grad_up, grad_down, dx_part = totals
    summed = lax.psum_scatter(
        dx_part.astype(jnp.bfloat16), "tensor", scatter_dimension=1, tiled=True
    )
    back_rows = lax.all_to_all(summed, "dp", split_axis=0, concat_axis=0, tiled=True)
    input_grad = contract(picked_tok, back_rows.reshape(-1, model_width), 0, 0).astype(jnp.bfloat16)
    return (
        input_grad,
        grad_gate.astype(jnp.bfloat16)[None],
        grad_up.astype(jnp.bfloat16)[None],
        grad_down.astype(jnp.bfloat16)[None],
    )


TILE = 512
ROWS = 16
PAIR = 256
MESH = pl.DeviceIdType.MESH


def fused_kernel(
    tok_hbm, cot_hbm, gates_hbm, routes_hbm, wg_hbm, wu_hbm, wd_hbm,
    dx_out, gst, ust, dst,
    gates_ref, routes_ref, xs, ys, wgu, wd, dgu, hid_t, dxb, sibr, hop1a, hop1b, hop2a, hop2b, zbuf,
    in_sem, w_sem, recv_sem, send_sem, zsend_sem, diag_sem,
    sib_send, sib_recv, h1_send, h1_recv, h2_send, h2_recv, zz_send, zz_recv,
):
    width = tok_hbm.shape[1]
    top = gates_hbm.shape[0]
    ff = wd.shape[0]
    half = width // 2
    dp = lax.axis_index("dp")
    y = lax.axis_index("tensor")
    z = lax.div(dp, 4)
    x = lax.rem(lax.div(dp, 2), 2)
    c = lax.rem(dp, 2)
    ox, oc, oy = 1 - x, 1 - c, 1 - y

    def dev(dz, dx, dc, dy):
        return ((dz * 2 + dx) * 2 + dc, dy)

    x_peer, y_peer, sib = dev(z, ox, c, y), dev(z, x, c, oy), dev(z, x, oc, y)
    odd = lax.rem(z, 2)
    low_side = z < 2
    inner = jnp.logical_or(z == 1, z == 2)
    outer = jnp.logical_or(z == 0, z == 3)
    z_at = [z, z + 1 - 2 * odd, jnp.where(low_side, 2, 1), jnp.where(low_side, 3, 0)]
    near, across = dev(z_at[1], x, c, y), dev(3 - z, x, c, y)
    z_peers = [dev(z_at[k], x, c, y) for k in range(1, 4)]
    own_half = jnp.where(low_side, 0, 2)
    halves = [own_half, 2 - own_half]

    barrier = pltpu.get_barrier_semaphore()
    for peer in [x_peer, y_peer, sib] + z_peers:
        pl.semaphore_signal(barrier, inc=1, device_id=peer, device_id_type=MESH)

    loads = [
        pltpu.make_async_copy(routes_hbm, routes_ref, in_sem.at[0]),
        pltpu.make_async_copy(gates_hbm, gates_ref, in_sem.at[1]),
        pltpu.make_async_copy(tok_hbm, xs.at[z, x, c, y, :, pl.ds(0, width)], in_sem.at[2]),
        pltpu.make_async_copy(cot_hbm, ys.at[z, x, c, y], in_sem.at[3]),
    ]
    weights = [
        pltpu.make_async_copy(wg_hbm.at[0], wgu.at[:, pl.ds(0, ff)], w_sem.at[0]),
        pltpu.make_async_copy(wu_hbm.at[0], wgu.at[:, pl.ds(ff, ff)], w_sem.at[1]),
        pltpu.make_async_copy(wd_hbm.at[0], wd, w_sem.at[2]),
    ]
    for copy in loads:
        copy.start()
    loads[0].wait()
    loads[1].wait()
    experts = lax.broadcasted_iota(jnp.int32, (128, ROWS), 0)
    turned = jnp.zeros((128, ROWS), jnp.float32)
    gate_vals = gates_ref[...].astype(jnp.float32)
    for k in range(top):
        turned = turned + jnp.where(routes_ref[k : k + 1, :] == experts, gate_vals[k : k + 1, :], 0.0)
    eye = lax.broadcasted_iota(jnp.int32, (ROWS, ROWS), 0) == lax.broadcasted_iota(jnp.int32, (ROWS, ROWS), 1)
    scale = contract(jnp.where(eye, 1.0, 0.0).astype(jnp.bfloat16), turned.astype(jnp.bfloat16), 1, 1)
    xs[z, x, c, y, :, pl.ds(width, 128)] = scale.astype(jnp.bfloat16)
    loads[2].wait()
    loads[3].wait()

    pl.semaphore_wait(barrier, 6)

    bufs = (xs, ys)
    pending = []
    inner_pending = []

    def copy_of(a, block, send, peer):
        bz, bx, bc, by = block
        view = bufs[a].at[bz, bx, bc, by]
        return pltpu.make_async_remote_copy(
            src_ref=view,
            dst_ref=view,
            send_sem=send,
            recv_sem=recv_sem.at[a, ((bz * 2 + bx) * 2 + bc) * 2 + by],
            device_id=peer,
            device_id_type=MESH,
        )

    def launch(copy):
        copy.start()
        pending.append(copy)

    def send(a, block, way, peer):
        bz, bx, bc, by = block
        launch(copy_of(a, block, send_sem.at[a, way, (bz * 2 + bx) * 2 + by], peer))

    def to_x(a, block):
        send(a, block, 0, x_peer)

    def to_y(a, block):
        send(a, block, 1, y_peer)

    def to_sib(a, block):
        send(a, block, 2, sib)

    def arrived(a, block):
        copy_of(a, block, send_sem.at[0, 0, 0], sib).wait_recv()

    def column(k):
        return (z_at[k], x, c, y)

    def own():
        block = column(0)
        to_x(0, block)
        to_y(1, block)
        for a in range(2):
            launch(copy_of(a, block, zsend_sem.at[a, 0], near))
        to_y(0, block)
        to_x(1, block)
        passed = [copy_of(a, block, zsend_sem.at[a, 1], across) for a in range(2)]

        @pl.when(inner)
        def _():
            for copy in passed:
                copy.start()

        inner_pending.extend(passed)
        for a in range(2):
            to_sib(a, block)

    def along(k, a):
        passed = copy_of(a, column(k), zsend_sem.at[a, 1 + k], across if k == 1 else near)

        @pl.when(inner)
        def _():
            arrived(a, column(k))
            passed.start()

        inner_pending.append(passed)

    def along_end(k, a):
        @pl.when(outer)
        def _():
            arrived(a, column(k))

    def spread(k, a):
        block = column(k)
        if k == 1 or a == 0:
            to_x(a, block)
        else:
            to_y(1, block)
            to_y(0, block)
            to_x(1, block)
        if k == 1:
            to_y(a, block)
        to_sib(a, block)

    def mid(k):
        block = (z_at[k], ox, c, y)
        arrived(0, block)
        if k != 1:
            to_y(0, block)
        to_sib(0, block)
        block = (z_at[k], x, c, oy)
        arrived(1, block)
        if k != 1:
            to_x(1, block)
        to_sib(1, block)

    def late(k):
        block = (z_at[k], x, c, oy)
        arrived(0, block)
        to_sib(0, block)
        block = (z_at[k], ox, c, y)
        arrived(1, block)
        to_sib(1, block)

    def corner(k):
        block = (z_at[k], ox, c, oy)
        for a in range(2):
            arrived(a, block)
            if k == 0:
                launch(copy_of(a, block, diag_sem.at[a], near))
            to_sib(a, block)

    def from_sib(a, k):
        for bx in (x, ox):
            for by in (y, oy):
                arrived(a, (z_at[k], bx, oc, by))

    def pair_rows(h):
        return pl.ds(pl.multiple_of(halves[h] * 128, PAIR), PAIR)

    def gate_up(h):
        xv = xs[pl.ds(halves[h], 2), :, :, :, :, pl.ds(0, width)].reshape(PAIR, width)
        return jnp.dot(xv, wgu[...], preferred_element_type=jnp.float32)

    def forward(h, pre):
        probs = xs[pl.ds(halves[h], 2), :, :, :, :, pl.ds(width, 128)].reshape(PAIR, 128).astype(jnp.float32)
        lane = lax.broadcasted_iota(jnp.int32, (PAIR, 128), 1)
        scale_rows = jnp.sum(jnp.where(lane == dp, probs, 0.0), axis=1, keepdims=True)
        yv = ys[pl.ds(halves[h], 2)].reshape(PAIR, width)
        gate_pre = pre[:, :ff]
        up_pre = pre[:, ff:]
        sig = jax.nn.sigmoid(gate_pre)
        act = gate_pre * sig
        hidden = jnp.where(scale_rows != 0.0, act * up_pre, 0.0)
        hid_t[:, pair_rows(h)] = hidden.T.astype(jnp.bfloat16)
        d_hidden = scale_rows * contract(yv, wd[...], 1, 1)
        d_gate = d_hidden * up_pre * sig * (1.0 + gate_pre * (1.0 - sig))
        dgu[pair_rows(h), pl.ds(0, ff)] = d_gate.astype(jnp.bfloat16)
        dgu[pair_rows(h), pl.ds(ff, ff)] = (d_hidden * act).astype(jnp.bfloat16)

    spans = (pl.ds(0, half), pl.ds(half, half))

    def remote(src, dst_ref, s_sem, r_sem, peer):
        return pltpu.make_async_remote_copy(
            src_ref=src, dst_ref=dst_ref, send_sem=s_sem, recv_sem=r_sem,
            device_id=peer, device_id_type=MESH,
        )

    def sib_hop(k, s):
        zk = z_at[k]
        return remote(
            dxb.at[zk, :, oc, :, :, spans[s]], sibr.at[zk, :, :, :, spans[s]],
            sib_send.at[k, s], sib_recv.at[k, s], sib,
        )

    def input_part(h, s):
        part = contract(dgu[pair_rows(h), :], wgu[spans[s], :], 1, 1)
        dxb[pl.ds(halves[h], 2), :, :, :, :, spans[s]] = part.astype(jnp.bfloat16).reshape(
            2, 2, 2, 2, ROWS, half
        )
        for k in ((1, 0), (3, 2))[h]:
            launch(sib_hop(k, s))

    def weight_grads(first, last):
        @pl.loop(first, last)
        def _(t):
            cols = pl.ds(pl.multiple_of(t * TILE, TILE), TILE)
            xt = xs[:, :, :, :, :, cols].reshape(32 * ROWS, TILE)
            both = contract(xt, dgu[...], 0, 0).astype(jnp.bfloat16)
            gst[0, cols, :] = both[:, :ff]
            ust[0, cols, :] = both[:, ff:]
            yt = ys[:, :, :, :, :, cols].reshape(32 * ROWS, TILE)
            dst[0, :, cols] = jnp.dot(hid_t[...], yt, preferred_element_type=jnp.float32).astype(jnp.bfloat16)

    def added(left, right):
        return (left.astype(jnp.float32) + right.astype(jnp.float32)).astype(jnp.bfloat16)

    def first_hop(h, k):
        zk = z_at[k]
        if h == 0:
            return remote(
                dxb.at[zk, :, c, oy, :, spans[0]], hop1a.at[zk],
                h1_send.at[0, k], h1_recv.at[0, k], y_peer,
            )
        return remote(
            dxb.at[zk, ox, c, :, :, spans[1]], hop1b.at[zk],
            h1_send.at[1, k], h1_recv.at[1, k], x_peer,
        )

    def second_hop(h, k):
        zk = z_at[k]
        if h == 0:
            return remote(
                dxb.at[zk, ox, c, y, :, spans[0]], hop2a.at[zk],
                h2_send.at[0, k], h2_recv.at[0, k], x_peer,
            )
        return remote(
            dxb.at[zk, x, c, oy, :, spans[1]], hop2b.at[zk],
            h2_send.at[1, k], h2_recv.at[1, k], y_peer,
        )

    def z_hop(k, slot):
        return remote(
            dxb.at[z_at[k], x, c, y], zbuf.at[slot],
            zz_send.at[k - 1], zz_recv.at[slot], dev(z_at[k], x, c, y),
        )

    def begin(k, s):
        zk = z_at[k]
        sib_hop(k, s).wait_recv()
        for bx in range(2):
            dxb[zk, bx, c, :, :, spans[s]] = added(
                dxb[zk, bx, c, :, :, spans[s]], sibr[zk, bx, :, :, spans[s]]
            )
        launch(first_hop(s, k))

    def middle(k):
        zk = z_at[k]
        first_hop(0, k).wait_recv()
        for bx in range(2):
            dxb[zk, bx, c, y, :, spans[0]] = added(dxb[zk, bx, c, y, :, spans[0]], hop1a[zk, bx])
        launch(second_hop(0, k))
        first_hop(1, k).wait_recv()
        for by in range(2):
            dxb[zk, x, c, by, :, spans[1]] = added(dxb[zk, x, c, by, :, spans[1]], hop1b[zk, by])
        launch(second_hop(1, k))

    def finish(k):
        zk = z_at[k]
        second_hop(0, k).wait_recv()
        dxb[zk, x, c, y, :, spans[0]] = added(dxb[zk, x, c, y, :, spans[0]], hop2a[zk])
        second_hop(1, k).wait_recv()
        dxb[zk, x, c, y, :, spans[1]] = added(dxb[zk, x, c, y, :, spans[1]], hop2b[zk])
        if k > 0:
            launch(z_hop(k, z))

    own()
    for copy in weights:
        copy.start()
    mid(0)
    along(1, 0)
    along_end(1, 0)
    spread(1, 0)
    along(2, 0)
    late(0)
    along(1, 1)
    along_end(1, 1)
    spread(1, 1)
    along(2, 1)
    corner(0)
    along(3, 0)
    along_end(2, 0)
    spread(2, 0)
    mid(1)
    along(3, 1)
    along_end(2, 1)
    spread(2, 1)
    late(1)
    along_end(3, 0)
    spread(3, 0)
    mid(2)
    along_end(3, 1)
    spread(3, 1)
    late(2)
    corner(1)
    for copy in weights:
        copy.wait()
    from_sib(0, 0)
    from_sib(0, 1)
    pre = gate_up(0)
    mid(3)
    corner(2)
    from_sib(1, 0)
    from_sib(1, 1)
    forward(0, pre)
    late(3)
    input_part(0, 0)
    corner(3)
    input_part(0, 1)
    begin(1, 0)
    begin(1, 1)
    from_sib(0, 2)
    from_sib(0, 3)
    pre = gate_up(1)
    begin(0, 0)
    begin(0, 1)
    from_sib(1, 2)
    from_sib(1, 3)
    forward(1, pre)
    middle(1)
    input_part(1, 0)
    input_part(1, 1)
    middle(0)
    begin(3, 0)
    begin(2, 0)
    begin(3, 1)
    begin(2, 1)
    finish(1)
    weight_grads(0, 2)
    middle(3)
    weight_grads(2, 3)
    middle(2)
    finish(3)
    weight_grads(3, 5)
    finish(2)
    finish(0)
    weight_grads(5, width // TILE)
    total = dxb[z, x, c, y].astype(jnp.float32)
    for k in range(1, 4):
        z_hop(k, z_at[k]).wait_recv()
        total = total + zbuf[z_at[k]].astype(jnp.float32)
    dx_out[...] = total.astype(jnp.bfloat16)

    for copy in pending:
        copy.wait_send()

    @pl.when(inner)
    def _():
        for copy in inner_pending:
            copy.wait_send()


def store_kernel(dx_ref, gg_ref, ug_ref, dg_ref, dx_out, gg_out, ug_out, dg_out, sem):
    copies = [pltpu.make_async_copy(dx_ref, dx_out, sem.at[0])]
    for ref, out in ((gg_ref, gg_out), (ug_ref, ug_out), (dg_ref, dg_out)):
        rows = ref.shape[1] // 4
        for part in range(4):
            span = pl.ds(part * rows, rows)
            copies.append(
                pltpu.make_async_copy(ref.at[0, span], out.at[0, span], sem.at[len(copies)])
            )
    for copy in copies:
        copy.start()
    for copy in copies:
        copy.wait()


def per_device_fused(tokens, cotangent, gates, routes, gate_weight, up_weight, down_weight):
    width = tokens.shape[1]
    ff = down_weight.shape[1]
    half = width // 2
    vmem = pl.BlockSpec(memory_space=pltpu.VMEM)
    hbm = pl.BlockSpec(memory_space=pltpu.HBM)
    low = jnp.bfloat16
    dma = pltpu.SemaphoreType.DMA
    outs = (
        jax.ShapeDtypeStruct(tokens.shape, low),
        jax.ShapeDtypeStruct(gate_weight.shape, low),
        jax.ShapeDtypeStruct(up_weight.shape, low),
        jax.ShapeDtypeStruct(down_weight.shape, low),
    )
    results = pl.pallas_call(
        fused_kernel,
        out_shape=outs,
        in_specs=[hbm] * 7,
        out_specs=(vmem, vmem, vmem, vmem),
        scratch_shapes=[
            pltpu.VMEM(gates.T.shape, low),
            pltpu.VMEM(routes.T.shape, jnp.int32),
            pltpu.VMEM((4, 2, 2, 2, ROWS, width + 128), low),
            pltpu.VMEM((4, 2, 2, 2, ROWS, width), low),
            pltpu.VMEM((width, 2 * ff), low),
            pltpu.VMEM((ff, width), low),
            pltpu.VMEM((32 * ROWS, 2 * ff), low),
            pltpu.VMEM((ff, 32 * ROWS), low),
            pltpu.VMEM((4, 2, 2, 2, ROWS, width), low),
            pltpu.VMEM((4, 2, 2, ROWS, width), low),
            pltpu.VMEM((4, 2, ROWS, half), low),
            pltpu.VMEM((4, 2, ROWS, half), low),
            pltpu.VMEM((4, ROWS, half), low),
            pltpu.VMEM((4, ROWS, half), low),
            pltpu.VMEM((4, ROWS, width), low),
            dma((4,)),
            dma((3,)),
            dma((2, 32)),
            dma((2, 3, 16)),
            dma((2, 5)),
            dma((2,)),
            dma((4, 2)),
            dma((4, 2)),
            dma((2, 4)),
            dma((2, 4)),
            dma((2, 4)),
            dma((2, 4)),
            dma((3,)),
            dma((4,)),
        ],
        compiler_params=pltpu.CompilerParams(
            collective_id=0, has_side_effects=True, vmem_limit_bytes=40 * 1024 * 1024
        ),
    )(tokens, cotangent, gates.T, routes.T, gate_weight, up_weight, down_weight)
    return pl.pallas_call(
        store_kernel,
        out_shape=outs,
        in_specs=[vmem] * 4,
        out_specs=(hbm,) * 4,
        scratch_shapes=[dma((13,))],
        compiler_params=pltpu.CompilerParams(vmem_limit_bytes=14 * 1024 * 1024),
    )(*results)


def is_slice_of_16(mesh):
    return mesh.shape["dp"] == 16 and mesh.shape["tensor"] == 2


def solution(mesh):
    per_device = per_device_fused if is_slice_of_16(mesh) else per_device_routed
    in_specs = (
        P(("dp", "tensor"), None),
        P(("dp", "tensor"), None),
        P(("dp", "tensor"), None),
        P(("dp", "tensor"), None),
        P("dp", None, "tensor"),
        P("dp", None, "tensor"),
        P("dp", "tensor", None),
    )
    out_specs = (
        P(("dp", "tensor"), None),
        P("dp", None, "tensor"),
        P("dp", None, "tensor"),
        P("dp", "tensor", None),
    )
    return jax.shard_map(
        per_device, mesh=mesh, in_specs=in_specs, out_specs=out_specs, check_vma=False
    )
```

```python
import jax
import jax.numpy as jnp
from jax import lax
from jax.experimental import pallas as pl
from jax.experimental.pallas import tpu as pltpu
from jax.sharding import PartitionSpec as P


def contract(left, right, left_dim, right_dim):
    return lax.dot_general(
        left, right, (((left_dim,), (right_dim,)), ((), ())), preferred_element_type=jnp.float32
    )


def per_device_routed(tokens, cotangent, gates, routes, gate_weight, up_weight, down_weight):
    dp_count = lax.axis_size("dp")
    tok_rows = tokens.shape[0]
    model_width = tokens.shape[1]
    top_count = routes.shape[1]
    capacity = min(tok_rows, tok_rows * top_count // dp_count + 1)
    w_gate = gate_weight[0]
    w_up = up_weight[0]
    w_down = down_weight[0]
    flat_routes = routes.reshape(-1)
    expert_ids = jnp.arange(dp_count, dtype=jnp.int32)
    route_table = (flat_routes[:, None] == expert_ids[None, :]).astype(jnp.int32)
    pair_ids = jnp.arange(flat_routes.shape[0], dtype=jnp.int32)
    earlier = (pair_ids[None, :] < pair_ids[:, None]).astype(jnp.bfloat16)
    route_rank = jnp.dot(
        earlier, route_table.astype(jnp.bfloat16), preferred_element_type=jnp.float32
    ).astype(jnp.int32)
    slot_index = jnp.sum(route_table * (expert_ids[None, :] * capacity + route_rank), axis=1)
    slot_ids = jnp.arange(dp_count * capacity, dtype=jnp.int32)
    picked = slot_index[None, :] == slot_ids[:, None]
    picked_tok = jnp.any(picked.reshape(dp_count * capacity, tok_rows, top_count), axis=2).astype(
        jnp.bfloat16
    )
    x_send = jnp.dot(picked_tok, tokens, preferred_element_type=jnp.float32).astype(jnp.bfloat16)
    dy_send = jnp.dot(picked_tok, cotangent, preferred_element_type=jnp.float32).astype(
        jnp.bfloat16
    )
    p_send = jnp.sum(
        jnp.where(picked, gates.reshape(-1)[None, :].astype(jnp.float32), jnp.float32(0.0)), axis=1
    )
    x_send = x_send.reshape(dp_count, 1, capacity, model_width)
    dy_send = dy_send.reshape(dp_count, 1, capacity, model_width)
    p_send = p_send.astype(jnp.bfloat16).reshape(dp_count, 1, capacity)
    grouped = (
        lax.all_gather(x_send, "tensor", axis=1, tiled=True),
        lax.all_gather(dy_send, "tensor", axis=1, tiled=True),
        lax.all_gather(p_send, "tensor", axis=1, tiled=True),
    )
    x_block = lax.all_to_all(grouped[0], "dp", split_axis=0, concat_axis=0, tiled=True)
    dy_block = lax.all_to_all(grouped[1], "dp", split_axis=0, concat_axis=0, tiled=True)
    p_block = lax.all_to_all(grouped[2], "dp", split_axis=0, concat_axis=0, tiled=True)
    lead_shape = x_block.shape[:3]
    x_rows = x_block.reshape(-1, model_width)
    dy_rows = dy_block.reshape(-1, model_width)
    scale_rows = p_block.reshape(-1).astype(jnp.float32)
    gate_pre = jnp.dot(x_rows, w_gate, preferred_element_type=jnp.float32)
    up_pre = jnp.dot(x_rows, w_up, preferred_element_type=jnp.float32)
    sig = jax.nn.sigmoid(gate_pre)
    act = gate_pre * sig
    hidden = (act * up_pre).astype(jnp.bfloat16)
    d_hidden = scale_rows[:, None] * contract(dy_rows, w_down, 1, 1)
    d_up = (d_hidden * act).astype(jnp.bfloat16)
    d_gate = (d_hidden * up_pre * sig * (1.0 + gate_pre * (1.0 - sig))).astype(jnp.bfloat16)
    grad_down = contract(hidden, dy_rows, 0, 0)
    grad_gate = contract(x_rows, d_gate, 0, 0)
    grad_up = contract(x_rows, d_up, 0, 0)
    dx_rows = contract(d_gate, w_gate, 1, 1) + contract(d_up, w_up, 1, 1)
    dx_rows = dx_rows.reshape(lead_shape + (model_width,))
    dx_part = dx_rows
    totals = (grad_gate, grad_up, grad_down, dx_part)
    grad_gate, grad_up, grad_down, dx_part = totals
    summed = lax.psum_scatter(
        dx_part.astype(jnp.bfloat16), "tensor", scatter_dimension=1, tiled=True
    )
    back_rows = lax.all_to_all(summed, "dp", split_axis=0, concat_axis=0, tiled=True)
    input_grad = contract(picked_tok, back_rows.reshape(-1, model_width), 0, 0).astype(jnp.bfloat16)
    return (
        input_grad,
        grad_gate.astype(jnp.bfloat16)[None],
        grad_up.astype(jnp.bfloat16)[None],
        grad_down.astype(jnp.bfloat16)[None],
    )


TILE = 512
ROWS = 16
PAIR = 256
ALONG_Z = (2,)
MESH = pl.DeviceIdType.MESH


def fused_kernel(
    tok_hbm, cot_hbm, gates_hbm, routes_hbm, wg_hbm, wu_hbm, wd_hbm,
    dx_out, gst, ust, dst,
    gates_ref, routes_ref, xs, ys, wgu, wd, dgu, hid_t, dxb, sibr, hop1a, hop1b, hop2a, hop2b, zbuf,
    in_sem, w_sem, recv_sem, send_sem, zsend_sem, diag_sem,
    sib_send, sib_recv, h1_send, h1_recv, h2_send, h2_recv, zz_send, zz_recv,
):
    width = tok_hbm.shape[1]
    top = gates_hbm.shape[0]
    ff = wd.shape[0]
    half = width // 2
    dp = lax.axis_index("dp")
    y = lax.axis_index("tensor")
    z = lax.div(dp, 4)
    x = lax.rem(lax.div(dp, 2), 2)
    c = lax.rem(dp, 2)
    ox, oc, oy = 1 - x, 1 - c, 1 - y

    def dev(dz, dx, dc, dy):
        return ((dz * 2 + dx) * 2 + dc, dy)

    x_peer, y_peer, sib = dev(z, ox, c, y), dev(z, x, c, oy), dev(z, x, oc, y)
    odd = lax.rem(z, 2)
    low_side = z < 2
    inner = jnp.logical_or(z == 1, z == 2)
    outer = jnp.logical_or(z == 0, z == 3)
    z_at = [z, z + 1 - 2 * odd, jnp.where(low_side, 2, 1), jnp.where(low_side, 3, 0)]
    near, across = dev(z_at[1], x, c, y), dev(3 - z, x, c, y)
    z_peers = [dev(z_at[k], x, c, y) for k in range(1, 4)]
    own_half = jnp.where(low_side, 0, 2)
    halves = [own_half, 2 - own_half]

    barrier = pltpu.get_barrier_semaphore()
    for peer in [x_peer, y_peer, sib] + z_peers:
        pl.semaphore_signal(barrier, inc=1, device_id=peer, device_id_type=MESH)

    loads = [
        pltpu.make_async_copy(routes_hbm, routes_ref, in_sem.at[0]),
        pltpu.make_async_copy(gates_hbm, gates_ref, in_sem.at[1]),
        pltpu.make_async_copy(tok_hbm, xs.at[z, x, c, y, :, pl.ds(0, width)], in_sem.at[2]),
        pltpu.make_async_copy(cot_hbm, ys.at[z, x, c, y], in_sem.at[3]),
    ]
    weights = [
        pltpu.make_async_copy(wg_hbm.at[0], wgu.at[:, pl.ds(0, ff)], w_sem.at[0]),
        pltpu.make_async_copy(wu_hbm.at[0], wgu.at[:, pl.ds(ff, ff)], w_sem.at[1]),
        pltpu.make_async_copy(wd_hbm.at[0], wd, w_sem.at[2]),
    ]
    for copy in loads:
        copy.start()
    loads[0].wait()
    loads[1].wait()
    experts = lax.broadcasted_iota(jnp.int32, (128, ROWS), 0)
    turned = jnp.zeros((128, ROWS), jnp.float32)
    gate_vals = gates_ref[...].astype(jnp.float32)
    for k in range(top):
        turned = turned + jnp.where(routes_ref[k : k + 1, :] == experts, gate_vals[k : k + 1, :], 0.0)
    eye = lax.broadcasted_iota(jnp.int32, (ROWS, ROWS), 0) == lax.broadcasted_iota(jnp.int32, (ROWS, ROWS), 1)
    scale = contract(jnp.where(eye, 1.0, 0.0).astype(jnp.bfloat16), turned.astype(jnp.bfloat16), 1, 1)
    xs[z, x, c, y, :, pl.ds(width, 128)] = scale.astype(jnp.bfloat16)
    loads[2].wait()
    loads[3].wait()

    pl.semaphore_wait(barrier, 6)

    bufs = (xs, ys)
    pending = []
    inner_pending = []

    def copy_of(a, block, send, peer):
        bz, bx, bc, by = block
        view = bufs[a].at[bz, bx, bc, by]
        return pltpu.make_async_remote_copy(
            src_ref=view,
            dst_ref=view,
            send_sem=send,
            recv_sem=recv_sem.at[a, ((bz * 2 + bx) * 2 + bc) * 2 + by],
            device_id=peer,
            device_id_type=MESH,
        )

    def launch(copy):
        copy.start()
        pending.append(copy)

    def send(a, block, way, peer):
        bz, bx, bc, by = block
        launch(copy_of(a, block, send_sem.at[a, way, (bz * 2 + bx) * 2 + by], peer))

    def to_x(a, block):
        send(a, block, 0, x_peer)

    def to_y(a, block):
        send(a, block, 1, y_peer)

    def to_sib(a, block):
        send(a, block, 2, sib)

    def arrived(a, block):
        copy_of(a, block, send_sem.at[0, 0, 0], sib).wait_recv()

    def column(k):
        return (z_at[k], x, c, y)

    def own_near(a):
        launch(copy_of(a, column(0), zsend_sem.at[a, 0], near))

    def own_across(a):
        passed = copy_of(a, column(0), zsend_sem.at[a, 1], across)
        inner_pending.append(passed)
        pl.when(inner)(passed.start)

    def along(k, a):
        passed = copy_of(a, column(k), zsend_sem.at[a, 1 + k], across if k == 1 else near)
        inner_pending.append(passed)

        @pl.when(inner)
        def _():
            arrived(a, column(k))
            passed.start()

    def along_end(k, a):
        @pl.when(outer)
        def _():
            arrived(a, column(k))

    def mid(k, a):
        block = (z_at[k], x, c, oy) if a else (z_at[k], ox, c, y)
        arrived(a, block)
        if k not in ALONG_Z:
            (to_x if a else to_y)(a, block)
        to_sib(a, block)

    def late(k, a):
        block = (z_at[k], ox, c, y) if a else (z_at[k], x, c, oy)
        arrived(a, block)
        to_sib(a, block)

    def corner_start(k, a):
        block = (z_at[k], ox, c, oy)
        passed = copy_of(a, block, diag_sem.at[a, 1 + k // 2], across if k == 0 else near)
        inner_pending.append(passed)

        @pl.when(inner)
        def _():
            arrived(a, block)
            passed.start()

    def corner(k, a):
        block = (z_at[k], ox, c, oy)
        if k in (0, 2) and 2 in ALONG_Z:

            @pl.when(outer)
            def _():
                arrived(a, block)

        else:
            arrived(a, block)
        if k == 0 and 1 in ALONG_Z:
            launch(copy_of(a, block, diag_sem.at[a, 0], near))
        to_sib(a, block)

    def from_sib(a, k):
        for bx in (x, ox):
            for by in (y, oy):
                arrived(a, (z_at[k], bx, oc, by))

    def rows_of(first, count):
        return pl.ds(pl.multiple_of(first * 128, 128), 128 * count)

    def gate_up(first, count):
        xv = xs[pl.ds(first, count), :, :, :, :, pl.ds(0, width)].reshape(128 * count, width)
        return jnp.dot(xv, wgu[...], preferred_element_type=jnp.float32)

    def forward(first, count, pre):
        rows = rows_of(first, count)
        probs = xs[pl.ds(first, count), :, :, :, :, pl.ds(width, 128)].reshape(128 * count, 128).astype(jnp.float32)
        lane = lax.broadcasted_iota(jnp.int32, (128 * count, 128), 1)
        scale_rows = jnp.sum(jnp.where(lane == dp, probs, 0.0), axis=1, keepdims=True)
        yv = ys[pl.ds(first, count)].reshape(128 * count, width)
        gate_pre = pre[:, :ff]
        up_pre = pre[:, ff:]
        sig = jax.nn.sigmoid(gate_pre)
        act = gate_pre * sig
        hidden = jnp.where(scale_rows != 0.0, act * up_pre, 0.0)
        hid_t[:, rows] = hidden.T.astype(jnp.bfloat16)
        d_hidden = scale_rows * contract(yv, wd[...], 1, 1)
        d_gate = d_hidden * up_pre * sig * (1.0 + gate_pre * (1.0 - sig))
        dgu[rows, pl.ds(0, ff)] = d_gate.astype(jnp.bfloat16)
        dgu[rows, pl.ds(ff, ff)] = (d_hidden * act).astype(jnp.bfloat16)

    spans = (pl.ds(0, half), pl.ds(half, half))

    def remote(src, dst_ref, s_sem, r_sem, peer):
        return pltpu.make_async_remote_copy(
            src_ref=src, dst_ref=dst_ref, send_sem=s_sem, recv_sem=r_sem,
            device_id=peer, device_id_type=MESH,
        )

    def sib_hop(k, s):
        zk = z_at[k]
        return remote(
            dxb.at[zk, :, oc, :, :, spans[s]], sibr.at[zk, :, :, :, spans[s]],
            sib_send.at[k, s], sib_recv.at[k, s], sib,
        )

    def input_part(first, count, s, ks):
        part = contract(dgu[rows_of(first, count), :], wgu[spans[s], :], 1, 1)
        dxb[pl.ds(first, count), :, :, :, :, spans[s]] = part.astype(jnp.bfloat16).reshape(
            count, 2, 2, 2, ROWS, half
        )
        for k in ks:
            launch(sib_hop(k, s))

    def weight_grads(first, last):
        @pl.loop(first, last)
        def _(t):
            cols = pl.ds(pl.multiple_of(t * TILE, TILE), TILE)
            xt = xs[:, :, :, :, :, cols].reshape(32 * ROWS, TILE)
            both = contract(xt, dgu[...], 0, 0).astype(jnp.bfloat16)
            gst[0, cols, :] = both[:, :ff]
            ust[0, cols, :] = both[:, ff:]
            yt = ys[:, :, :, :, :, cols].reshape(32 * ROWS, TILE)
            dst[0, :, cols] = jnp.dot(hid_t[...], yt, preferred_element_type=jnp.float32).astype(jnp.bfloat16)

    def added(left, right):
        return (left.astype(jnp.float32) + right.astype(jnp.float32)).astype(jnp.bfloat16)

    def first_hop(h, k):
        zk = z_at[k]
        if h == 0:
            return remote(
                dxb.at[zk, :, c, oy, :, spans[0]], hop1a.at[zk],
                h1_send.at[0, k], h1_recv.at[0, k], y_peer,
            )
        return remote(
            dxb.at[zk, ox, c, :, :, spans[1]], hop1b.at[zk],
            h1_send.at[1, k], h1_recv.at[1, k], x_peer,
        )

    def second_hop(h, k):
        zk = z_at[k]
        if h == 0:
            return remote(
                dxb.at[zk, ox, c, y, :, spans[0]], hop2a.at[zk],
                h2_send.at[0, k], h2_recv.at[0, k], x_peer,
            )
        return remote(
            dxb.at[zk, x, c, oy, :, spans[1]], hop2b.at[zk],
            h2_send.at[1, k], h2_recv.at[1, k], y_peer,
        )

    def z_hop(k, slot):
        return remote(
            dxb.at[z_at[k], x, c, y], zbuf.at[slot],
            zz_send.at[k - 1], zz_recv.at[slot], dev(z_at[k], x, c, y),
        )

    def begin(k, s):
        zk = z_at[k]
        sib_hop(k, s).wait_recv()
        for bx in range(2):
            dxb[zk, bx, c, :, :, spans[s]] = added(
                dxb[zk, bx, c, :, :, spans[s]], sibr[zk, bx, :, :, spans[s]]
            )
        launch(first_hop(s, k))

    def middle(k, h):
        zk = z_at[k]
        first_hop(h, k).wait_recv()
        for b in range(2):
            if h == 0:
                dxb[zk, b, c, y, :, spans[0]] = added(dxb[zk, b, c, y, :, spans[0]], hop1a[zk, b])
            else:
                dxb[zk, x, c, b, :, spans[1]] = added(dxb[zk, x, c, b, :, spans[1]], hop1b[zk, b])
        launch(second_hop(h, k))

    def finish(k, h):
        zk = z_at[k]
        second_hop(h, k).wait_recv()
        hop = hop2b if h else hop2a
        dxb[zk, x, c, y, :, spans[h]] = added(dxb[zk, x, c, y, :, spans[h]], hop[zk])

    to_x(0, column(0))
    to_y(1, column(0))
    own_across(0)
    own_near(0)
    to_sib(0, column(0))
    to_y(0, column(0))
    to_x(1, column(0))
    own_near(1)
    own_across(1)
    along_end(1, 0)
    mid(0, 0)
    along(1, 0)
    mid(0, 1)
    to_sib(0, column(1))
    along(2, 0)
    along_end(1, 1)
    to_sib(1, column(0))
    along(1, 1)
    to_y(1, column(1))
    to_x(0, column(1))
    for copy in weights:
        copy.start()
    to_x(1, column(1))
    to_y(0, column(1))
    along(3, 0)
    along_end(3, 0)
    to_sib(1, column(1))
    corner_start(0, 1)
    to_x(0, column(3))
    mid(1, 0)
    along(3, 1)
    mid(1, 1)
    late(0, 0)
    along_end(3, 1)
    for copy in weights:
        copy.wait()
    corner(0, 1)
    corner_start(0, 0)
    along(2, 1)
    to_y(1, column(3))
    corner(0, 0)
    late(0, 1)
    along_end(2, 0)
    to_y(0, column(3))
    from_sib(1, 0)
    to_x(0, column(2))
    to_sib(0, column(3))
    from_sib(0, 0)
    mid(3, 0)
    late(1, 1)
    to_y(0, column(2))
    late(1, 0)
    along_end(2, 1)
    corner(1, 0)
    corner_start(2, 1)
    to_x(1, column(3))
    to_sib(1, column(2))
    to_sib(0, column(2))
    corner_start(2, 0)
    to_sib(1, column(3))
    from_sib(0, 1)
    to_y(1, column(2))
    corner(1, 1)
    pre_a = gate_up(own_half, 2)
    mid(3, 1)
    from_sib(1, 1)
    forward(own_half, 2, pre_a)
    to_x(1, column(2))
    mid(2, 0)
    input_part(own_half, 2, 1, (1, 0))
    late(3, 0)
    corner(3, 0)
    input_part(own_half, 2, 0, (1, 0))
    begin(0, 1)
    corner(2, 1)
    from_sib(0, 3)
    corner(2, 0)
    late(3, 1)
    begin(1, 1)
    corner(3, 1)
    late(2, 0)
    pre_3 = gate_up(z_at[3], 1)
    begin(1, 0)
    from_sib(1, 3)
    from_sib(0, 2)
    begin(0, 0)
    forward(z_at[3], 1, pre_3)
    input_part(z_at[3], 1, 1, (3,))
    input_part(z_at[3], 1, 0, (3,))
    begin(3, 1)
    mid(2, 1)
    late(2, 1)
    pre_2 = gate_up(z_at[2], 1)
    begin(3, 0)
    middle(1, 0)
    from_sib(1, 2)
    forward(z_at[2], 1, pre_2)
    input_part(z_at[2], 1, 0, (2,))
    input_part(z_at[2], 1, 1, (2,))
    middle(3, 1)
    middle(3, 0)
    begin(2, 0)
    middle(1, 1)
    begin(2, 1)
    weight_grads(0, 2)
    finish(3, 0)
    finish(3, 1)
    launch(z_hop(3, z))
    finish(1, 0)
    weight_grads(2, 3)
    middle(2, 0)
    middle(2, 1)
    middle(0, 1)
    finish(1, 1)
    launch(z_hop(1, z))
    weight_grads(3, 4)
    middle(0, 0)
    finish(2, 0)
    finish(2, 1)
    launch(z_hop(2, z))
    weight_grads(4, 6)
    finish(0, 1)
    finish(0, 0)
    weight_grads(6, 7)
    total = dxb[z, x, c, y].astype(jnp.float32)
    for k in range(1, 4):
        z_hop(k, z_at[k]).wait_recv()
        total = total + zbuf[z_at[k]].astype(jnp.float32)
    dx_out[...] = total.astype(jnp.bfloat16)

    for copy in pending:
        copy.wait_send()

    @pl.when(inner)
    def _():
        for copy in inner_pending:
            copy.wait_send()


def store_kernel(dx_ref, gg_ref, ug_ref, dg_ref, dx_out, gg_out, ug_out, dg_out, sem):
    copies = [pltpu.make_async_copy(dx_ref, dx_out, sem.at[0])]
    for ref, out in ((gg_ref, gg_out), (ug_ref, ug_out), (dg_ref, dg_out)):
        rows = ref.shape[1] // 4
        for part in range(4):
            span = pl.ds(part * rows, rows)
            copies.append(
                pltpu.make_async_copy(ref.at[0, span], out.at[0, span], sem.at[len(copies)])
            )
    for copy in copies:
        copy.start()
    for copy in copies:
        copy.wait()


def per_device_fused(tokens, cotangent, gates, routes, gate_weight, up_weight, down_weight):
    width = tokens.shape[1]
    ff = down_weight.shape[1]
    half = width // 2
    vmem = pl.BlockSpec(memory_space=pltpu.VMEM)
    hbm = pl.BlockSpec(memory_space=pltpu.HBM)
    low = jnp.bfloat16
    dma = pltpu.SemaphoreType.DMA
    outs = (
        jax.ShapeDtypeStruct(tokens.shape, low),
        jax.ShapeDtypeStruct(gate_weight.shape, low),
        jax.ShapeDtypeStruct(up_weight.shape, low),
        jax.ShapeDtypeStruct(down_weight.shape, low),
    )
    results = pl.pallas_call(
        fused_kernel,
        out_shape=outs,
        in_specs=[hbm] * 7,
        out_specs=(vmem, vmem, vmem, vmem),
        scratch_shapes=[
            pltpu.VMEM(gates.T.shape, low),
            pltpu.VMEM(routes.T.shape, jnp.int32),
            pltpu.VMEM((4, 2, 2, 2, ROWS, width + 128), low),
            pltpu.VMEM((4, 2, 2, 2, ROWS, width), low),
            pltpu.VMEM((width, 2 * ff), low),
            pltpu.VMEM((ff, width), low),
            pltpu.VMEM((32 * ROWS, 2 * ff), low),
            pltpu.VMEM((ff, 32 * ROWS), low),
            pltpu.VMEM((4, 2, 2, 2, ROWS, width), low),
            pltpu.VMEM((4, 2, 2, ROWS, width), low),
            pltpu.VMEM((4, 2, ROWS, half), low),
            pltpu.VMEM((4, 2, ROWS, half), low),
            pltpu.VMEM((4, ROWS, half), low),
            pltpu.VMEM((4, ROWS, half), low),
            pltpu.VMEM((4, ROWS, width), low),
            dma((4,)),
            dma((3,)),
            dma((2, 32)),
            dma((2, 3, 16)),
            dma((2, 5)),
            dma((2, 3)),
            dma((4, 2)),
            dma((4, 2)),
            dma((2, 4)),
            dma((2, 4)),
            dma((2, 4)),
            dma((2, 4)),
            dma((3,)),
            dma((4,)),
        ],
        compiler_params=pltpu.CompilerParams(
            collective_id=0, has_side_effects=True, vmem_limit_bytes=40 * 1024 * 1024
        ),
    )(*[pltpu.with_memory_space_constraint(a, pltpu.HBM) for a in (tokens, cotangent, gates.T, routes.T, gate_weight, up_weight, down_weight)])
    return pl.pallas_call(
        store_kernel,
        out_shape=outs,
        in_specs=[vmem] * 4,
        out_specs=(hbm,) * 4,
        scratch_shapes=[dma((13,))],
        compiler_params=pltpu.CompilerParams(vmem_limit_bytes=14 * 1024 * 1024),
    )(*results)


def is_slice_of_16(mesh):
    return mesh.shape["dp"] == 16 and mesh.shape["tensor"] == 2


def solution(mesh):
    per_device = per_device_fused if is_slice_of_16(mesh) else per_device_routed
    in_specs = (
        P(("dp", "tensor"), None),
        P(("dp", "tensor"), None),
        P(("dp", "tensor"), None),
        P(("dp", "tensor"), None),
        P("dp", None, "tensor"),
        P("dp", None, "tensor"),
        P("dp", "tensor", None),
    )
    out_specs = (
        P(("dp", "tensor"), None),
        P("dp", None, "tensor"),
        P("dp", None, "tensor"),
        P("dp", "tensor", None),
    )
    return jax.shard_map(
        per_device, mesh=mesh, in_specs=in_specs, out_specs=out_specs, check_vma=False
    )
```

```python
import jax
import jax.numpy as jnp
from jax import lax
from jax.experimental import pallas as pl
from jax.experimental.pallas import tpu as pltpu
from jax.sharding import PartitionSpec as P


def contract(left, right, left_dim, right_dim):
    return lax.dot_general(
        left, right, (((left_dim,), (right_dim,)), ((), ())), preferred_element_type=jnp.float32
    )


def per_device_routed(tokens, cotangent, gates, routes, gate_weight, up_weight, down_weight):
    dp_count = lax.axis_size("dp")
    tok_rows = tokens.shape[0]
    model_width = tokens.shape[1]
    top_count = routes.shape[1]
    capacity = min(tok_rows, tok_rows * top_count // dp_count + 1)
    w_gate = gate_weight[0]
    w_up = up_weight[0]
    w_down = down_weight[0]
    flat_routes = routes.reshape(-1)
    expert_ids = jnp.arange(dp_count, dtype=jnp.int32)
    route_table = (flat_routes[:, None] == expert_ids[None, :]).astype(jnp.int32)
    pair_ids = jnp.arange(flat_routes.shape[0], dtype=jnp.int32)
    earlier = (pair_ids[None, :] < pair_ids[:, None]).astype(jnp.bfloat16)
    route_rank = jnp.dot(
        earlier, route_table.astype(jnp.bfloat16), preferred_element_type=jnp.float32
    ).astype(jnp.int32)
    slot_index = jnp.sum(route_table * (expert_ids[None, :] * capacity + route_rank), axis=1)
    slot_ids = jnp.arange(dp_count * capacity, dtype=jnp.int32)
    picked = slot_index[None, :] == slot_ids[:, None]
    picked_tok = jnp.any(picked.reshape(dp_count * capacity, tok_rows, top_count), axis=2).astype(
        jnp.bfloat16
    )
    x_send = jnp.dot(picked_tok, tokens, preferred_element_type=jnp.float32).astype(jnp.bfloat16)
    dy_send = jnp.dot(picked_tok, cotangent, preferred_element_type=jnp.float32).astype(
        jnp.bfloat16
    )
    p_send = jnp.sum(
        jnp.where(picked, gates.reshape(-1)[None, :].astype(jnp.float32), jnp.float32(0.0)), axis=1
    )
    x_send = x_send.reshape(dp_count, 1, capacity, model_width)
    dy_send = dy_send.reshape(dp_count, 1, capacity, model_width)
    p_send = p_send.astype(jnp.bfloat16).reshape(dp_count, 1, capacity)
    grouped = (
        lax.all_gather(x_send, "tensor", axis=1, tiled=True),
        lax.all_gather(dy_send, "tensor", axis=1, tiled=True),
        lax.all_gather(p_send, "tensor", axis=1, tiled=True),
    )
    x_block = lax.all_to_all(grouped[0], "dp", split_axis=0, concat_axis=0, tiled=True)
    dy_block = lax.all_to_all(grouped[1], "dp", split_axis=0, concat_axis=0, tiled=True)
    p_block = lax.all_to_all(grouped[2], "dp", split_axis=0, concat_axis=0, tiled=True)
    lead_shape = x_block.shape[:3]
    x_rows = x_block.reshape(-1, model_width)
    dy_rows = dy_block.reshape(-1, model_width)
    scale_rows = p_block.reshape(-1).astype(jnp.float32)
    gate_pre = jnp.dot(x_rows, w_gate, preferred_element_type=jnp.float32)
    up_pre = jnp.dot(x_rows, w_up, preferred_element_type=jnp.float32)
    sig = jax.nn.sigmoid(gate_pre)
    act = gate_pre * sig
    hidden = (act * up_pre).astype(jnp.bfloat16)
    d_hidden = scale_rows[:, None] * contract(dy_rows, w_down, 1, 1)
    d_up = (d_hidden * act).astype(jnp.bfloat16)
    d_gate = (d_hidden * up_pre * sig * (1.0 + gate_pre * (1.0 - sig))).astype(jnp.bfloat16)
    grad_down = contract(hidden, dy_rows, 0, 0)
    grad_gate = contract(x_rows, d_gate, 0, 0)
    grad_up = contract(x_rows, d_up, 0, 0)
    dx_rows = contract(d_gate, w_gate, 1, 1) + contract(d_up, w_up, 1, 1)
    dx_rows = dx_rows.reshape(lead_shape + (model_width,))
    dx_part = dx_rows
    totals = (grad_gate, grad_up, grad_down, dx_part)
    grad_gate, grad_up, grad_down, dx_part = totals
    summed = lax.psum_scatter(
        dx_part.astype(jnp.bfloat16), "tensor", scatter_dimension=1, tiled=True
    )
    back_rows = lax.all_to_all(summed, "dp", split_axis=0, concat_axis=0, tiled=True)
    input_grad = contract(picked_tok, back_rows.reshape(-1, model_width), 0, 0).astype(jnp.bfloat16)
    return (
        input_grad,
        grad_gate.astype(jnp.bfloat16)[None],
        grad_up.astype(jnp.bfloat16)[None],
        grad_down.astype(jnp.bfloat16)[None],
    )


TILE = 512
ROWS = 16
PAIR = 256
ALONG_Z = (2,)
MESH = pl.DeviceIdType.MESH


def fused_kernel(
    tok_hbm, cot_hbm, gates_hbm, routes_hbm, wg_hbm, wu_hbm, wd_hbm,
    dx_out, gst, ust, dst,
    gates_ref, routes_ref, xs, ys, wgu, wd, dgu, hid_t, dxb, sibr, hop1a, hop1b, hop2a, hop2b, zbuf, nearr,
    in_sem, w_sem, recv_sem, send_sem, zsend_sem, diag_sem,
    sib_send, sib_recv, h1_send, h1_recv, h2_send, h2_recv, zz_send, zz_recv, near_send, near_recv,
):
    width = tok_hbm.shape[1]
    top = gates_hbm.shape[0]
    ff = wd.shape[0]
    half = width // 2
    dp = lax.axis_index("dp")
    y = lax.axis_index("tensor")
    z = lax.div(dp, 4)
    x = lax.rem(lax.div(dp, 2), 2)
    c = lax.rem(dp, 2)
    ox, oc, oy = 1 - x, 1 - c, 1 - y

    def dev(dz, dx, dc, dy):
        return ((dz * 2 + dx) * 2 + dc, dy)

    x_peer, y_peer, sib = dev(z, ox, c, y), dev(z, x, c, oy), dev(z, x, oc, y)
    odd = lax.rem(z, 2)
    low_side = z < 2
    inner = jnp.logical_or(z == 1, z == 2)
    outer = jnp.logical_or(z == 0, z == 3)
    z_at = [z, z + 1 - 2 * odd, jnp.where(low_side, 2, 1), jnp.where(low_side, 3, 0)]
    near, across = dev(z_at[1], x, c, y), dev(3 - z, x, c, y)
    z_peers = [dev(z_at[k], x, c, y) for k in range(1, 4)]
    own_half = jnp.where(low_side, 0, 2)
    halves = [own_half, 2 - own_half]

    barrier = pltpu.get_barrier_semaphore()
    for peer in [x_peer, y_peer, sib] + z_peers:
        pl.semaphore_signal(barrier, inc=1, device_id=peer, device_id_type=MESH)

    loads = [
        pltpu.make_async_copy(routes_hbm, routes_ref, in_sem.at[0]),
        pltpu.make_async_copy(gates_hbm, gates_ref, in_sem.at[1]),
        pltpu.make_async_copy(tok_hbm, xs.at[z, x, c, y, :, pl.ds(0, width)], in_sem.at[2]),
        pltpu.make_async_copy(cot_hbm, ys.at[z, x, c, y], in_sem.at[3]),
    ]
    weights = [
        pltpu.make_async_copy(wg_hbm.at[0], wgu.at[:, pl.ds(0, ff)], w_sem.at[0]),
        pltpu.make_async_copy(wu_hbm.at[0], wgu.at[:, pl.ds(ff, ff)], w_sem.at[1]),
        pltpu.make_async_copy(wd_hbm.at[0], wd, w_sem.at[2]),
    ]
    for copy in loads:
        copy.start()
    pl.semaphore_wait(barrier, 6)

    bufs = (xs, ys)
    pending = []
    inner_pending = []
    last_pending = []

    def copy_of(a, block, send, peer, src=None):
        bz, bx, bc, by = block
        view = bufs[a].at[bz, bx, bc, by]
        return pltpu.make_async_remote_copy(
            src_ref=view if src is None else src,
            dst_ref=view,
            send_sem=send,
            recv_sem=recv_sem.at[a, ((bz * 2 + bx) * 2 + bc) * 2 + by],
            device_id=peer,
            device_id_type=MESH,
        )

    def launch(copy):
        copy.start()
        pending.append(copy)

    def send(a, block, way, peer, src=None):
        bz, bx, bc, by = block
        launch(copy_of(a, block, send_sem.at[a, way, (bz * 2 + bx) * 2 + by], peer, src))

    def own_to(way, a):
        send(a, column(0), way, (x_peer, y_peer, sib)[way], cot_hbm if a else None)

    def to_x(a, block):
        send(a, block, 0, x_peer)

    def to_y(a, block):
        send(a, block, 1, y_peer)

    def to_sib(a, block):
        send(a, block, 2, sib)

    def arrived(a, block):
        copy_of(a, block, send_sem.at[0, 0, 0], sib).wait_recv()

    def column(k):
        return (z_at[k], x, c, y)

    def own_rows():
        loads[0].wait()
        loads[1].wait()
        experts = lax.broadcasted_iota(jnp.int32, (128, ROWS), 0)
        turned = jnp.zeros((128, ROWS), jnp.float32)
        gate_vals = gates_ref[...].astype(jnp.float32)
        for k in range(top):
            turned = turned + jnp.where(routes_ref[k : k + 1, :] == experts, gate_vals[k : k + 1, :], 0.0)
        eye = lax.broadcasted_iota(jnp.int32, (ROWS, ROWS), 0) == lax.broadcasted_iota(jnp.int32, (ROWS, ROWS), 1)
        scale = contract(jnp.where(eye, 1.0, 0.0).astype(jnp.bfloat16), turned.astype(jnp.bfloat16), 1, 1)
        xs[z, x, c, y, :, pl.ds(width, 128)] = scale.astype(jnp.bfloat16)
        loads[2].wait()
        loads[3].wait()

    def send_home(k):
        copy = z_hop(k, z)
        copy.start()
        last_pending.append(copy)

    def own_near(a):
        launch(copy_of(a, column(0), zsend_sem.at[a, 0], near, cot_hbm if a else None))

    def own_across(a):
        passed = copy_of(a, column(0), zsend_sem.at[a, 1], across, cot_hbm if a else None)
        inner_pending.append(passed)
        pl.when(inner)(passed.start)

    def along(k, a):
        passed = copy_of(a, column(k), zsend_sem.at[a, 1 + k], across if k == 1 else near)
        inner_pending.append(passed)

        @pl.when(inner)
        def _():
            arrived(a, column(k))
            passed.start()

    def along_end(k, a):
        @pl.when(outer)
        def _():
            arrived(a, column(k))

    def mid(k, a):
        block = (z_at[k], x, c, oy) if a else (z_at[k], ox, c, y)
        arrived(a, block)
        if k not in ALONG_Z:
            (to_x if a else to_y)(a, block)
        to_sib(a, block)

    def late(k, a):
        block = (z_at[k], ox, c, y) if a else (z_at[k], x, c, oy)
        arrived(a, block)
        to_sib(a, block)

    def corner_start(k, a):
        block = (z_at[k], ox, c, oy)
        passed = copy_of(a, block, diag_sem.at[a, 1 + k // 2], across if k == 0 else near)
        inner_pending.append(passed)

        @pl.when(inner)
        def _():
            arrived(a, block)
            passed.start()

    def corner(k, a):
        block = (z_at[k], ox, c, oy)
        if k in (0, 2) and 2 in ALONG_Z:

            @pl.when(outer)
            def _():
                arrived(a, block)

        else:
            arrived(a, block)
        if k == 0 and 1 in ALONG_Z:
            launch(copy_of(a, block, diag_sem.at[a, 0], near))
        to_sib(a, block)

    def from_sib(a, k):
        for bx in (x, ox):
            for by in (y, oy):
                arrived(a, (z_at[k], bx, oc, by))

    def rows_of(first, count):
        return pl.ds(pl.multiple_of(first * 128, 128), 128 * count)

    def gate_up(first, count):
        xv = xs[pl.ds(first, count), :, :, :, :, pl.ds(0, width)].reshape(128 * count, width)
        return jnp.dot(xv, wgu[...], preferred_element_type=jnp.float32)

    def forward(first, count, pre):
        rows = rows_of(first, count)
        probs = xs[pl.ds(first, count), :, :, :, :, pl.ds(width, 128)].reshape(128 * count, 128).astype(jnp.float32)
        lane = lax.broadcasted_iota(jnp.int32, (128 * count, 128), 1)
        scale_rows = jnp.sum(jnp.where(lane == dp, probs, 0.0), axis=1, keepdims=True)
        yv = ys[pl.ds(first, count)].reshape(128 * count, width)
        gate_pre = pre[:, :ff]
        up_pre = pre[:, ff:]
        sig = jax.nn.sigmoid(gate_pre)
        act = gate_pre * sig
        hidden = jnp.where(scale_rows != 0.0, act * up_pre, 0.0)
        hid_t[:, rows] = hidden.T.astype(jnp.bfloat16)
        d_hidden = scale_rows * contract(yv, wd[...], 1, 1)
        d_gate = d_hidden * up_pre * sig * (1.0 + gate_pre * (1.0 - sig))
        dgu[rows, pl.ds(0, ff)] = d_gate.astype(jnp.bfloat16)
        dgu[rows, pl.ds(ff, ff)] = (d_hidden * act).astype(jnp.bfloat16)

    spans = (pl.ds(0, half), pl.ds(half, half))

    def remote(src, dst_ref, s_sem, r_sem, peer):
        return pltpu.make_async_remote_copy(
            src_ref=src, dst_ref=dst_ref, send_sem=s_sem, recv_sem=r_sem,
            device_id=peer, device_id_type=MESH,
        )

    def sib_hop(k, s):
        zk = z_at[k]
        return remote(
            dxb.at[zk, :, oc, :, :, spans[s]], sibr.at[zk, :, :, :, spans[s]],
            sib_send.at[k, s], sib_recv.at[k, s], sib,
        )

    def input_part(first, count, s, ks):
        part = contract(dgu[rows_of(first, count), :], wgu[spans[s], :], 1, 1)
        dxb[pl.ds(first, count), :, :, :, :, spans[s]] = part.astype(jnp.bfloat16).reshape(
            count, 2, 2, 2, ROWS, half
        )
        for k in ks:
            launch(sib_hop(k, s))

    def weight_grads(first, last):
        @pl.loop(first, last)
        def _(t):
            cols = pl.ds(pl.multiple_of(t * TILE, TILE), TILE)
            xt = xs[:, :, :, :, :, cols].reshape(32 * ROWS, TILE)
            both = contract(xt, dgu[...], 0, 0).astype(jnp.bfloat16)
            gst[0, cols, :] = both[:, :ff]
            ust[0, cols, :] = both[:, ff:]
            yt = ys[:, :, :, :, :, cols].reshape(32 * ROWS, TILE)
            dst[0, :, cols] = jnp.dot(hid_t[...], yt, preferred_element_type=jnp.float32).astype(jnp.bfloat16)

    def added(left, right):
        return (left.astype(jnp.float32) + right.astype(jnp.float32)).astype(jnp.bfloat16)

    def first_hop(h, k):
        zk = z_at[k]
        if h == 0:
            return remote(
                dxb.at[zk, :, c, oy, :, spans[0]], hop1a.at[zk],
                h1_send.at[0, k], h1_recv.at[0, k], y_peer,
            )
        return remote(
            dxb.at[zk, ox, c, :, :, spans[1]], hop1b.at[zk],
            h1_send.at[1, k], h1_recv.at[1, k], x_peer,
        )

    def second_hop(h, k):
        zk = z_at[k]
        if h == 0:
            return remote(
                dxb.at[zk, ox, c, y, :, spans[0]], hop2a.at[zk],
                h2_send.at[0, k], h2_recv.at[0, k], x_peer,
            )
        return remote(
            dxb.at[zk, x, c, oy, :, spans[1]], hop2b.at[zk],
            h2_send.at[1, k], h2_recv.at[1, k], y_peer,
        )

    def z_hop(k, slot):
        return remote(
            dxb.at[z_at[k], x, c, y], zbuf.at[slot],
            zz_send.at[k - 2], zz_recv.at[slot], dev(z_at[k], x, c, y),
        )

    def near_hop(s):
        return remote(
            dxb.at[z_at[1], :, c, :, :, spans[s]], nearr.at[:, :, :, spans[s]],
            near_send.at[s], near_recv.at[s], near,
        )

    def begin(k, s):
        zk = z_at[k]
        sib_hop(k, s).wait_recv()
        for bx in range(2):
            dxb[zk, bx, c, :, :, spans[s]] = added(
                dxb[zk, bx, c, :, :, spans[s]], sibr[zk, bx, :, :, spans[s]]
            )
        launch(near_hop(s) if k == 1 else first_hop(s, k))

    def begin_own(s):
        sib_hop(0, s).wait_recv()
        near_hop(s).wait_recv()
        for bx in range(2):
            pair = dxb[z, bx, c, :, :, spans[s]].astype(jnp.float32) + sibr[z, bx, :, :, spans[s]].astype(jnp.float32)
            dxb[z, bx, c, :, :, spans[s]] = (pair + nearr[bx, :, :, spans[s]].astype(jnp.float32)).astype(jnp.bfloat16)
        launch(first_hop(s, 0))

    def middle(k, h):
        zk = z_at[k]
        first_hop(h, k).wait_recv()
        for b in range(2):
            if h == 0:
                dxb[zk, b, c, y, :, spans[0]] = added(dxb[zk, b, c, y, :, spans[0]], hop1a[zk, b])
            else:
                dxb[zk, x, c, b, :, spans[1]] = added(dxb[zk, x, c, b, :, spans[1]], hop1b[zk, b])
        launch(second_hop(h, k))

    def finish(k, h):
        zk = z_at[k]
        second_hop(h, k).wait_recv()
        hop = hop2b if h else hop2a
        dxb[zk, x, c, y, :, spans[h]] = added(dxb[zk, x, c, y, :, spans[h]], hop[zk])

    own_across(1)
    own_to(1, 1)
    own_near(1)
    own_to(0, 1)
    own_rows()
    for copy in weights:
        copy.start()
    own_near(0)
    own_to(1, 0)
    own_to(0, 0)
    along(1, 1)
    along_end(1, 1)
    to_y(1, column(1))
    mid(0, 1)
    along(2, 1)
    late(0, 1)
    along(1, 0)
    late(0, 0)
    along_end(1, 0)
    mid(0, 0)
    for copy in weights:
        copy.wait()
    to_x(0, column(1))
    to_x(1, column(1))
    along(3, 1)
    own_to(2, 0)
    to_y(0, column(1))
    corner_start(0, 1)
    own_across(0)
    along_end(2, 1)
    to_sib(0, column(1))
    along(3, 0)
    corner_start(0, 0)
    mid(1, 1)
    corner(0, 0)
    mid(1, 0)
    own_to(2, 1)
    to_sib(1, column(1))
    corner(0, 1)
    from_sib(0, 0)
    pre_0 = gate_up(z_at[0], 1)
    along_end(3, 1)
    corner_start(2, 1)
    from_sib(1, 0)
    to_y(1, column(3))
    late(1, 1)
    along(2, 0)
    forward(z_at[0], 1, pre_0)
    along_end(3, 0)
    to_sib(1, column(2))
    to_x(0, column(3))
    late(1, 0)
    to_sib(1, column(3))
    to_x(1, column(3))
    to_sib(0, column(3))
    to_y(0, column(3))
    corner(1, 0)
    input_part(z_at[0], 1, 0, (0,))
    corner_start(2, 0)
    from_sib(0, 1)
    corner(1, 1)
    pre_1 = gate_up(z_at[1], 1)
    mid(3, 1)
    from_sib(1, 1)
    mid(3, 0)
    forward(z_at[1], 1, pre_1)
    input_part(z_at[1], 1, 1, (1,))
    input_part(z_at[1], 1, 0, (1,))
    along_end(2, 0)
    to_x(0, column(2))
    late(3, 0)
    begin(1, 1)
    corner(3, 0)
    late(3, 1)
    to_sib(0, column(2))
    corner(3, 1)
    to_y(0, column(2))
    corner(2, 0)
    to_y(1, column(2))
    corner(2, 1)
    to_x(1, column(2))
    begin(1, 0)
    from_sib(0, 3)
    pre_3 = gate_up(z_at[3], 1)
    from_sib(1, 3)
    forward(z_at[3], 1, pre_3)
    input_part(z_at[3], 1, 1, (3,))
    late(2, 0)
    mid(2, 0)
    input_part(z_at[3], 1, 0, (3,))
    begin(3, 1)
    late(2, 1)
    from_sib(0, 2)
    mid(2, 1)
    pre_2 = gate_up(z_at[2], 1)
    begin(3, 0)
    from_sib(1, 2)
    forward(z_at[2], 1, pre_2)
    input_part(z_at[2], 1, 0, (2,))
    middle(3, 1)
    input_part(z_at[2], 1, 1, (2,))
    middle(3, 0)
    begin(2, 0)
    begin_own(0)
    begin(2, 1)
    input_part(z_at[0], 1, 1, (0,))
    finish(3, 0)
    finish(3, 1)
    send_home(3)
    weight_grads(0, 1)
    middle(2, 0)
    begin_own(1)
    middle(2, 1)
    weight_grads(1, 3)
    finish(2, 0)
    middle(0, 0)
    finish(2, 1)
    send_home(2)
    weight_grads(3, 4)
    middle(0, 1)
    weight_grads(4, 5)
    finish(0, 0)
    weight_grads(5, 7)
    finish(0, 1)
    for copy in pending:
        copy.wait_send()

    @pl.when(inner)
    def _():
        for copy in inner_pending:
            copy.wait_send()

    total = dxb[z, x, c, y].astype(jnp.float32)
    for k in range(2, 4):
        z_hop(k, z_at[k]).wait_recv()
        total = total + zbuf[z_at[k]].astype(jnp.float32)
    dx_out[...] = total.astype(jnp.bfloat16)

    for copy in last_pending:
        copy.wait_send()


def store_kernel(dx_ref, gg_ref, ug_ref, dg_ref, dx_out, gg_out, ug_out, dg_out, sem):
    copies = [pltpu.make_async_copy(dx_ref, dx_out, sem.at[0])]
    for ref, out in ((gg_ref, gg_out), (ug_ref, ug_out), (dg_ref, dg_out)):
        rows = ref.shape[1] // 4
        for part in range(4):
            span = pl.ds(part * rows, rows)
            copies.append(
                pltpu.make_async_copy(ref.at[0, span], out.at[0, span], sem.at[len(copies)])
            )
    for copy in copies:
        copy.start()
    for copy in copies:
        copy.wait()


def per_device_fused(tokens, cotangent, gates, routes, gate_weight, up_weight, down_weight):
    width = tokens.shape[1]
    ff = down_weight.shape[1]
    half = width // 2
    vmem = pl.BlockSpec(memory_space=pltpu.VMEM)
    hbm = pl.BlockSpec(memory_space=pltpu.HBM)
    low = jnp.bfloat16
    dma = pltpu.SemaphoreType.DMA
    outs = (
        jax.ShapeDtypeStruct(tokens.shape, low),
        jax.ShapeDtypeStruct(gate_weight.shape, low),
        jax.ShapeDtypeStruct(up_weight.shape, low),
        jax.ShapeDtypeStruct(down_weight.shape, low),
    )
    operands = (tokens, cotangent, gates.T, routes.T, gate_weight, up_weight, down_weight)
    results = pl.pallas_call(
        fused_kernel,
        out_shape=outs,
        in_specs=[hbm] * 7,
        out_specs=(vmem, vmem, vmem, vmem),
        scratch_shapes=[
            pltpu.VMEM(gates.T.shape, low),
            pltpu.VMEM(routes.T.shape, jnp.int32),
            pltpu.VMEM((4, 2, 2, 2, ROWS, width + 128), low),
            pltpu.VMEM((4, 2, 2, 2, ROWS, width), low),
            pltpu.VMEM((width, 2 * ff), low),
            pltpu.VMEM((ff, width), low),
            pltpu.VMEM((32 * ROWS, 2 * ff), low),
            pltpu.VMEM((ff, 32 * ROWS), low),
            pltpu.VMEM((4, 2, 2, 2, ROWS, width), low),
            pltpu.VMEM((4, 2, 2, ROWS, width), low),
            pltpu.VMEM((4, 2, ROWS, half), low),
            pltpu.VMEM((4, 2, ROWS, half), low),
            pltpu.VMEM((4, ROWS, half), low),
            pltpu.VMEM((4, ROWS, half), low),
            pltpu.VMEM((4, ROWS, width), low),
            pltpu.VMEM((2, 2, ROWS, width), low),
            dma((4,)),
            dma((3,)),
            dma((2, 32)),
            dma((2, 3, 16)),
            dma((2, 5)),
            dma((2, 3)),
            dma((4, 2)),
            dma((4, 2)),
            dma((2, 4)),
            dma((2, 4)),
            dma((2, 4)),
            dma((2, 4)),
            dma((2,)),
            dma((4,)),
            dma((2,)),
            dma((2,)),
        ],
        compiler_params=pltpu.CompilerParams(
            collective_id=0, has_side_effects=True, vmem_limit_bytes=40 * 1024 * 1024
        ),
    )(*[pltpu.with_memory_space_constraint(a, pltpu.HBM) for a in operands])
    return pl.pallas_call(
        store_kernel,
        out_shape=outs,
        in_specs=[vmem] * 4,
        out_specs=(hbm,) * 4,
        scratch_shapes=[dma((13,))],
        compiler_params=pltpu.CompilerParams(vmem_limit_bytes=14 * 1024 * 1024),
    )(*results)


def is_slice_of_16(mesh):
    return mesh.shape["dp"] == 16 and mesh.shape["tensor"] == 2


def solution(mesh):
    per_device = per_device_fused if is_slice_of_16(mesh) else per_device_routed
    in_specs = (
        P(("dp", "tensor"), None),
        P(("dp", "tensor"), None),
        P(("dp", "tensor"), None),
        P(("dp", "tensor"), None),
        P("dp", None, "tensor"),
        P("dp", None, "tensor"),
        P("dp", "tensor", None),
    )
    out_specs = (
        P(("dp", "tensor"), None),
        P("dp", None, "tensor"),
        P("dp", None, "tensor"),
        P("dp", "tensor", None),
    )
    return jax.shard_map(
        per_device, mesh=mesh, in_specs=in_specs, out_specs=out_specs, check_vma=False
    )
```

```python
import jax
import jax.numpy as jnp
from jax import lax
from jax.experimental import pallas as pl
from jax.experimental.pallas import tpu as pltpu
from jax.sharding import PartitionSpec as P


def contract(left, right, left_dim, right_dim):
    return lax.dot_general(
        left, right, (((left_dim,), (right_dim,)), ((), ())), preferred_element_type=jnp.float32
    )


def per_device_routed(tokens, cotangent, gates, routes, gate_weight, up_weight, down_weight):
    dp_count = lax.axis_size("dp")
    tok_rows = tokens.shape[0]
    model_width = tokens.shape[1]
    top_count = routes.shape[1]
    capacity = min(tok_rows, tok_rows * top_count // dp_count + 1)
    w_gate = gate_weight[0]
    w_up = up_weight[0]
    w_down = down_weight[0]
    flat_routes = routes.reshape(-1)
    expert_ids = jnp.arange(dp_count, dtype=jnp.int32)
    route_table = (flat_routes[:, None] == expert_ids[None, :]).astype(jnp.int32)
    pair_ids = jnp.arange(flat_routes.shape[0], dtype=jnp.int32)
    earlier = (pair_ids[None, :] < pair_ids[:, None]).astype(jnp.bfloat16)
    route_rank = jnp.dot(
        earlier, route_table.astype(jnp.bfloat16), preferred_element_type=jnp.float32
    ).astype(jnp.int32)
    slot_index = jnp.sum(route_table * (expert_ids[None, :] * capacity + route_rank), axis=1)
    slot_ids = jnp.arange(dp_count * capacity, dtype=jnp.int32)
    picked = slot_index[None, :] == slot_ids[:, None]
    picked_tok = jnp.any(picked.reshape(dp_count * capacity, tok_rows, top_count), axis=2).astype(
        jnp.bfloat16
    )
    x_send = jnp.dot(picked_tok, tokens, preferred_element_type=jnp.float32).astype(jnp.bfloat16)
    dy_send = jnp.dot(picked_tok, cotangent, preferred_element_type=jnp.float32).astype(
        jnp.bfloat16
    )
    p_send = jnp.sum(
        jnp.where(picked, gates.reshape(-1)[None, :].astype(jnp.float32), jnp.float32(0.0)), axis=1
    )
    x_send = x_send.reshape(dp_count, 1, capacity, model_width)
    dy_send = dy_send.reshape(dp_count, 1, capacity, model_width)
    p_send = p_send.astype(jnp.bfloat16).reshape(dp_count, 1, capacity)
    grouped = (
        lax.all_gather(x_send, "tensor", axis=1, tiled=True),
        lax.all_gather(dy_send, "tensor", axis=1, tiled=True),
        lax.all_gather(p_send, "tensor", axis=1, tiled=True),
    )
    x_block = lax.all_to_all(grouped[0], "dp", split_axis=0, concat_axis=0, tiled=True)
    dy_block = lax.all_to_all(grouped[1], "dp", split_axis=0, concat_axis=0, tiled=True)
    p_block = lax.all_to_all(grouped[2], "dp", split_axis=0, concat_axis=0, tiled=True)
    lead_shape = x_block.shape[:3]
    x_rows = x_block.reshape(-1, model_width)
    dy_rows = dy_block.reshape(-1, model_width)
    scale_rows = p_block.reshape(-1).astype(jnp.float32)
    gate_pre = jnp.dot(x_rows, w_gate, preferred_element_type=jnp.float32)
    up_pre = jnp.dot(x_rows, w_up, preferred_element_type=jnp.float32)
    sig = jax.nn.sigmoid(gate_pre)
    act = gate_pre * sig
    hidden = (act * up_pre).astype(jnp.bfloat16)
    d_hidden = scale_rows[:, None] * contract(dy_rows, w_down, 1, 1)
    d_up = (d_hidden * act).astype(jnp.bfloat16)
    d_gate = (d_hidden * up_pre * sig * (1.0 + gate_pre * (1.0 - sig))).astype(jnp.bfloat16)
    grad_down = contract(hidden, dy_rows, 0, 0)
    grad_gate = contract(x_rows, d_gate, 0, 0)
    grad_up = contract(x_rows, d_up, 0, 0)
    dx_rows = contract(d_gate, w_gate, 1, 1) + contract(d_up, w_up, 1, 1)
    dx_rows = dx_rows.reshape(lead_shape + (model_width,))
    dx_part = dx_rows
    totals = (grad_gate, grad_up, grad_down, dx_part)
    grad_gate, grad_up, grad_down, dx_part = totals
    summed = lax.psum_scatter(
        dx_part.astype(jnp.bfloat16), "tensor", scatter_dimension=1, tiled=True
    )
    back_rows = lax.all_to_all(summed, "dp", split_axis=0, concat_axis=0, tiled=True)
    input_grad = contract(picked_tok, back_rows.reshape(-1, model_width), 0, 0).astype(jnp.bfloat16)
    return (
        input_grad,
        grad_gate.astype(jnp.bfloat16)[None],
        grad_up.astype(jnp.bfloat16)[None],
        grad_down.astype(jnp.bfloat16)[None],
    )


TILE = 512
ROWS = 16
PAIR = 256
ALONG_Z = (2,)
MESH = pl.DeviceIdType.MESH


def fused_kernel(
    tok_hbm, cot_hbm, gates_hbm, routes_hbm, wg_hbm, wu_hbm, wd_hbm,
    dx_out, gst, ust, dst,
    gates_ref, routes_ref, xs, ys, wgu, wd, dgu, hid_t, dxb, sibr, hop1a, hop1b, hop2a, hop2b, zbuf, nearr,
    in_sem, w_sem, recv_sem, send_sem, zsend_sem, diag_sem,
    sib_send, sib_recv, h1_send, h1_recv, h2_send, h2_recv, zz_send, zz_recv, near_send, near_recv,
):
    width = tok_hbm.shape[1]
    top = gates_hbm.shape[0]
    ff = wd.shape[0]
    half = width // 2
    dp = lax.axis_index("dp")
    y = lax.axis_index("tensor")
    z = lax.div(dp, 4)
    x = lax.rem(lax.div(dp, 2), 2)
    c = lax.rem(dp, 2)
    ox, oc, oy = 1 - x, 1 - c, 1 - y

    def dev(dz, dx, dc, dy):
        return ((dz * 2 + dx) * 2 + dc, dy)

    x_peer, y_peer, sib = dev(z, ox, c, y), dev(z, x, c, oy), dev(z, x, oc, y)
    odd = lax.rem(z, 2)
    low_side = z < 2
    inner = jnp.logical_or(z == 1, z == 2)
    outer = jnp.logical_or(z == 0, z == 3)
    z_at = [z, z + 1 - 2 * odd, jnp.where(low_side, 2, 1), jnp.where(low_side, 3, 0)]
    near, across = dev(z_at[1], x, c, y), dev(3 - z, x, c, y)
    z_peers = [dev(z_at[k], x, c, y) for k in range(1, 4)]
    own_half = jnp.where(low_side, 0, 2)
    halves = [own_half, 2 - own_half]

    barrier = pltpu.get_barrier_semaphore()
    for peer in [x_peer, y_peer, sib] + z_peers:
        pl.semaphore_signal(barrier, inc=1, device_id=peer, device_id_type=MESH)

    loads = [
        pltpu.make_async_copy(routes_hbm, routes_ref, in_sem.at[0]),
        pltpu.make_async_copy(gates_hbm, gates_ref, in_sem.at[1]),
        pltpu.make_async_copy(tok_hbm, xs.at[z, x, c, y, :, pl.ds(0, width)], in_sem.at[2]),
        pltpu.make_async_copy(cot_hbm, ys.at[z, x, c, y], in_sem.at[3]),
    ]
    weights = [
        pltpu.make_async_copy(wg_hbm.at[0], wgu.at[:, pl.ds(0, ff)], w_sem.at[0]),
        pltpu.make_async_copy(wu_hbm.at[0], wgu.at[:, pl.ds(ff, ff)], w_sem.at[1]),
        pltpu.make_async_copy(wd_hbm.at[0], wd, w_sem.at[2]),
    ]
    for copy in loads:
        copy.start()
    pl.semaphore_wait(barrier, 6)

    bufs = (xs, ys)
    pending = []
    inner_pending = []
    last_pending = []

    def copy_of(a, block, send, peer, src=None):
        bz, bx, bc, by = block
        view = bufs[a].at[bz, bx, bc, by]
        return pltpu.make_async_remote_copy(
            src_ref=view if src is None else src,
            dst_ref=view,
            send_sem=send,
            recv_sem=recv_sem.at[a, ((bz * 2 + bx) * 2 + bc) * 2 + by],
            device_id=peer,
            device_id_type=MESH,
        )

    def launch(copy):
        copy.start()
        pending.append(copy)

    def send(a, block, way, peer, src=None):
        bz, bx, bc, by = block
        launch(copy_of(a, block, send_sem.at[a, way, (bz * 2 + bx) * 2 + by], peer, src))

    def own_to(way, a):
        send(a, column(0), way, (x_peer, y_peer, sib)[way], cot_hbm if a else None)

    def to_x(a, block):
        send(a, block, 0, x_peer)

    def to_y(a, block):
        send(a, block, 1, y_peer)

    def to_sib(a, block):
        send(a, block, 2, sib)

    def arrived(a, block):
        copy_of(a, block, send_sem.at[0, 0, 0], sib).wait_recv()

    def column(k):
        return (z_at[k], x, c, y)

    def own_rows():
        loads[0].wait()
        loads[1].wait()
        experts = lax.broadcasted_iota(jnp.int32, (128, ROWS), 0)
        turned = jnp.zeros((128, ROWS), jnp.float32)
        gate_vals = gates_ref[...].astype(jnp.float32)
        for k in range(top):
            turned = turned + jnp.where(routes_ref[k : k + 1, :] == experts, gate_vals[k : k + 1, :], 0.0)
        eye = lax.broadcasted_iota(jnp.int32, (ROWS, ROWS), 0) == lax.broadcasted_iota(jnp.int32, (ROWS, ROWS), 1)
        scale = contract(jnp.where(eye, 1.0, 0.0).astype(jnp.bfloat16), turned.astype(jnp.bfloat16), 1, 1)
        xs[z, x, c, y, :, pl.ds(width, 128)] = scale.astype(jnp.bfloat16)
        loads[2].wait()
        loads[3].wait()

    def send_home(k):
        copy = z_hop(k, z)
        copy.start()
        last_pending.append(copy)

    def own_near(a):
        launch(copy_of(a, column(0), zsend_sem.at[a, 0], near, cot_hbm if a else None))

    def own_across(a):
        passed = copy_of(a, column(0), zsend_sem.at[a, 1], across, cot_hbm if a else None)
        inner_pending.append(passed)
        pl.when(inner)(passed.start)

    def along(k, a):
        passed = copy_of(a, column(k), zsend_sem.at[a, 1 + k], across if k == 1 else near)
        inner_pending.append(passed)

        @pl.when(inner)
        def _():
            arrived(a, column(k))
            passed.start()

    def along_end(k, a):
        @pl.when(outer)
        def _():
            arrived(a, column(k))

    def mid(k, a):
        block = (z_at[k], x, c, oy) if a else (z_at[k], ox, c, y)
        arrived(a, block)
        if k not in ALONG_Z:
            (to_x if a else to_y)(a, block)
        to_sib(a, block)

    def late(k, a):
        block = (z_at[k], ox, c, y) if a else (z_at[k], x, c, oy)
        arrived(a, block)
        to_sib(a, block)

    def corner_start(k, a):
        block = (z_at[k], ox, c, oy)
        passed = copy_of(a, block, diag_sem.at[a, 1 + k // 2], across if k == 0 else near)
        inner_pending.append(passed)

        @pl.when(inner)
        def _():
            arrived(a, block)
            passed.start()

    def corner(k, a):
        block = (z_at[k], ox, c, oy)
        if k in (0, 2) and 2 in ALONG_Z:

            @pl.when(outer)
            def _():
                arrived(a, block)

        else:
            arrived(a, block)
        if k == 0 and 1 in ALONG_Z:
            launch(copy_of(a, block, diag_sem.at[a, 0], near))
        to_sib(a, block)

    def from_sib(a, k):
        for bx in (x, ox):
            for by in (y, oy):
                arrived(a, (z_at[k], bx, oc, by))

    def rows_of(first, count):
        return pl.ds(pl.multiple_of(first * 128, 128), 128 * count)

    def gate_up(first, count):
        xv = xs[pl.ds(first, count), :, :, :, :, pl.ds(0, width)].reshape(128 * count, width)
        return jnp.dot(xv, wgu[...], preferred_element_type=jnp.float32)

    def forward(first, count, pre):
        rows = rows_of(first, count)
        probs = xs[pl.ds(first, count), :, :, :, :, pl.ds(width, 128)].reshape(128 * count, 128).astype(jnp.float32)
        lane = lax.broadcasted_iota(jnp.int32, (128 * count, 128), 1)
        scale_rows = jnp.sum(jnp.where(lane == dp, probs, 0.0), axis=1, keepdims=True)
        yv = ys[pl.ds(first, count)].reshape(128 * count, width)
        gate_pre = pre[:, :ff]
        up_pre = pre[:, ff:]
        sig = jax.nn.sigmoid(gate_pre)
        act = gate_pre * sig
        hidden = jnp.where(scale_rows != 0.0, act * up_pre, 0.0)
        hid_t[:, rows] = hidden.T.astype(jnp.bfloat16)
        d_hidden = scale_rows * contract(yv, wd[...], 1, 1)
        d_gate = d_hidden * up_pre * sig * (1.0 + gate_pre * (1.0 - sig))
        dgu[rows, pl.ds(0, ff)] = d_gate.astype(jnp.bfloat16)
        dgu[rows, pl.ds(ff, ff)] = (d_hidden * act).astype(jnp.bfloat16)

    spans = (pl.ds(0, half), pl.ds(half, half))

    def remote(src, dst_ref, s_sem, r_sem, peer):
        return pltpu.make_async_remote_copy(
            src_ref=src, dst_ref=dst_ref, send_sem=s_sem, recv_sem=r_sem,
            device_id=peer, device_id_type=MESH,
        )

    def sib_hop(k, s):
        zk = z_at[k]
        return remote(
            dxb.at[zk, :, oc, :, :, spans[s]], sibr.at[zk, :, :, :, spans[s]],
            sib_send.at[k, s], sib_recv.at[k, s], sib,
        )

    def input_part(first, count, s, ks):
        part = contract(dgu[rows_of(first, count), :], wgu[spans[s], :], 1, 1)
        dxb[pl.ds(first, count), :, :, :, :, spans[s]] = part.astype(jnp.bfloat16).reshape(
            count, 2, 2, 2, ROWS, half
        )
        for k in ks:
            launch(sib_hop(k, s))

    def weight_grads(first, last):
        @pl.loop(first, last)
        def _(t):
            cols = pl.ds(pl.multiple_of(t * TILE, TILE), TILE)
            xt = xs[:, :, :, :, :, cols].reshape(32 * ROWS, TILE)
            both = contract(xt, dgu[...], 0, 0).astype(jnp.bfloat16)
            gst[0, cols, :] = both[:, :ff]
            ust[0, cols, :] = both[:, ff:]
            yt = ys[:, :, :, :, :, cols].reshape(32 * ROWS, TILE)
            dst[0, :, cols] = jnp.dot(hid_t[...], yt, preferred_element_type=jnp.float32).astype(jnp.bfloat16)

    def added(left, right):
        return (left.astype(jnp.float32) + right.astype(jnp.float32)).astype(jnp.bfloat16)

    def first_hop(h, k):
        zk = z_at[k]
        if h == 0:
            return remote(
                dxb.at[zk, :, c, oy, :, spans[0]], hop1a.at[zk],
                h1_send.at[0, k], h1_recv.at[0, k], y_peer,
            )
        return remote(
            dxb.at[zk, ox, c, :, :, spans[1]], hop1b.at[zk],
            h1_send.at[1, k], h1_recv.at[1, k], x_peer,
        )

    def second_hop(h, k):
        zk = z_at[k]
        if h == 0:
            return remote(
                dxb.at[zk, ox, c, y, :, spans[0]], hop2a.at[zk],
                h2_send.at[0, k], h2_recv.at[0, k], x_peer,
            )
        return remote(
            dxb.at[zk, x, c, oy, :, spans[1]], hop2b.at[zk],
            h2_send.at[1, k], h2_recv.at[1, k], y_peer,
        )

    def z_hop(k, slot):
        return remote(
            dxb.at[z_at[k], x, c, y], zbuf.at[slot],
            zz_send.at[k - 2], zz_recv.at[slot], dev(z_at[k], x, c, y),
        )

    def near_hop(s):
        return remote(
            dxb.at[z_at[1], :, c, :, :, spans[s]], nearr.at[:, :, :, spans[s]],
            near_send.at[s], near_recv.at[s], near,
        )

    def begin(k, s):
        zk = z_at[k]
        sib_hop(k, s).wait_recv()
        for bx in range(2):
            dxb[zk, bx, c, :, :, spans[s]] = added(
                dxb[zk, bx, c, :, :, spans[s]], sibr[zk, bx, :, :, spans[s]]
            )
        launch(near_hop(s) if k == 1 else first_hop(s, k))

    def begin_own(s):
        sib_hop(0, s).wait_recv()
        near_hop(s).wait_recv()
        for bx in range(2):
            pair = dxb[z, bx, c, :, :, spans[s]].astype(jnp.float32) + sibr[z, bx, :, :, spans[s]].astype(jnp.float32)
            dxb[z, bx, c, :, :, spans[s]] = (pair + nearr[bx, :, :, spans[s]].astype(jnp.float32)).astype(jnp.bfloat16)
        launch(first_hop(s, 0))

    def middle(k, h):
        zk = z_at[k]
        first_hop(h, k).wait_recv()
        for b in range(2):
            if h == 0:
                dxb[zk, b, c, y, :, spans[0]] = added(dxb[zk, b, c, y, :, spans[0]], hop1a[zk, b])
            else:
                dxb[zk, x, c, b, :, spans[1]] = added(dxb[zk, x, c, b, :, spans[1]], hop1b[zk, b])
        launch(second_hop(h, k))

    def finish(k, h):
        zk = z_at[k]
        second_hop(h, k).wait_recv()
        hop = hop2b if h else hop2a
        dxb[zk, x, c, y, :, spans[h]] = added(dxb[zk, x, c, y, :, spans[h]], hop[zk])

    own_to(1, 1)
    own_near(1)
    own_to(0, 1)
    own_rows()
    own_to(1, 0)
    own_across(1)
    own_near(0)
    own_to(0, 0)
    along_end(1, 1)
    along(1, 1)
    mid(0, 1)
    to_y(1, column(1))
    for copy in weights:
        copy.start()
    along(2, 1)
    along_end(1, 0)
    along(1, 0)
    to_x(0, column(1))
    to_y(0, column(1))
    along(3, 1)
    for copy in weights:
        copy.wait()
    mid(0, 0)
    own_to(2, 1)
    to_sib(1, column(1))
    own_to(2, 0)
    corner_start(0, 1)
    to_x(1, column(1))
    along_end(2, 1)
    along(3, 0)
    late(0, 1)
    mid(1, 0)
    mid(1, 1)
    corner(0, 1)
    own_across(0)
    late(0, 0)
    along_end(3, 1)
    to_sib(1, column(2))
    corner_start(2, 1)
    corner_start(0, 0)
    from_sib(1, 0)
    to_y(1, column(3))
    to_sib(0, column(1))
    late(1, 1)
    corner(0, 0)
    to_sib(1, column(3))
    along_end(3, 0)
    to_x(0, column(3))
    late(1, 0)
    to_x(1, column(3))
    along(2, 0)
    corner(1, 0)
    from_sib(0, 0)
    to_y(0, column(3))
    corner(1, 1)
    to_sib(0, column(3))
    from_sib(0, 1)
    pre_a = gate_up(own_half, 2)
    from_sib(1, 1)
    mid(3, 1)
    corner_start(2, 0)
    mid(3, 0)
    forward(own_half, 2, pre_a)
    late(3, 0)
    input_part(own_half, 2, 0, (1, 0))
    input_part(own_half, 2, 1, (1, 0))
    begin(1, 0)
    corner(3, 0)
    late(3, 1)
    along_end(2, 0)
    corner(2, 0)
    to_y(0, column(2))
    to_y(1, column(2))
    to_sib(0, column(2))
    to_x(0, column(2))
    corner(3, 1)
    corner(2, 1)
    begin(1, 1)
    to_x(1, column(2))
    from_sib(0, 3)
    pre_3 = gate_up(z_at[3], 1)
    from_sib(1, 3)
    forward(z_at[3], 1, pre_3)
    input_part(z_at[3], 1, 1, (3,))
    late(2, 0)
    mid(2, 0)
    input_part(z_at[3], 1, 0, (3,))
    from_sib(0, 2)
    late(2, 1)
    begin(3, 1)
    mid(2, 1)
    pre_2 = gate_up(z_at[2], 1)
    begin(3, 0)
    from_sib(1, 2)
    forward(z_at[2], 1, pre_2)
    input_part(z_at[2], 1, 0, (2,))
    middle(3, 1)
    input_part(z_at[2], 1, 1, (2,))
    middle(3, 0)
    begin(2, 0)
    begin(2, 1)
    finish(3, 1)
    begin_own(0)
    weight_grads(0, 1)
    finish(3, 0)
    send_home(3)
    weight_grads(1, 2)
    middle(2, 0)
    begin_own(1)
    middle(2, 1)
    weight_grads(2, 4)
    finish(2, 0)
    middle(0, 0)
    finish(2, 1)
    send_home(2)
    weight_grads(4, 5)
    middle(0, 1)
    weight_grads(5, 6)
    finish(0, 0)
    weight_grads(6, 7)
    finish(0, 1)
    for copy in pending:
        copy.wait_send()

    @pl.when(inner)
    def _():
        for copy in inner_pending:
            copy.wait_send()

    total = dxb[z, x, c, y].astype(jnp.float32)
    for k in range(2, 4):
        z_hop(k, z_at[k]).wait_recv()
        total = total + zbuf[z_at[k]].astype(jnp.float32)
    dx_out[...] = total.astype(jnp.bfloat16)

    for copy in last_pending:
        copy.wait_send()


def store_kernel(dx_ref, gg_ref, ug_ref, dg_ref, dx_out, gg_out, ug_out, dg_out, sem):
    copies = [pltpu.make_async_copy(dx_ref, dx_out, sem.at[0])]
    for ref, out in ((gg_ref, gg_out), (ug_ref, ug_out), (dg_ref, dg_out)):
        rows = ref.shape[1] // 4
        for part in range(4):
            span = pl.ds(part * rows, rows)
            copies.append(
                pltpu.make_async_copy(ref.at[0, span], out.at[0, span], sem.at[len(copies)])
            )
    for copy in copies:
        copy.start()
    for copy in copies:
        copy.wait()


def per_device_fused(tokens, cotangent, gates, routes, gate_weight, up_weight, down_weight):
    width = tokens.shape[1]
    ff = down_weight.shape[1]
    half = width // 2
    vmem = pl.BlockSpec(memory_space=pltpu.VMEM)
    hbm = pl.BlockSpec(memory_space=pltpu.HBM)
    low = jnp.bfloat16
    dma = pltpu.SemaphoreType.DMA
    outs = (
        jax.ShapeDtypeStruct(tokens.shape, low),
        jax.ShapeDtypeStruct(gate_weight.shape, low),
        jax.ShapeDtypeStruct(up_weight.shape, low),
        jax.ShapeDtypeStruct(down_weight.shape, low),
    )
    operands = (tokens, cotangent, gates.T, routes.T, gate_weight, up_weight, down_weight)
    results = pl.pallas_call(
        fused_kernel,
        out_shape=outs,
        in_specs=[hbm] * 7,
        out_specs=(vmem, vmem, vmem, vmem),
        scratch_shapes=[
            pltpu.VMEM(gates.T.shape, low),
            pltpu.VMEM(routes.T.shape, jnp.int32),
            pltpu.VMEM((4, 2, 2, 2, ROWS, width + 128), low),
            pltpu.VMEM((4, 2, 2, 2, ROWS, width), low),
            pltpu.VMEM((width, 2 * ff), low),
            pltpu.VMEM((ff, width), low),
            pltpu.VMEM((32 * ROWS, 2 * ff), low),
            pltpu.VMEM((ff, 32 * ROWS), low),
            pltpu.VMEM((4, 2, 2, 2, ROWS, width), low),
            pltpu.VMEM((4, 2, 2, ROWS, width), low),
            pltpu.VMEM((4, 2, ROWS, half), low),
            pltpu.VMEM((4, 2, ROWS, half), low),
            pltpu.VMEM((4, ROWS, half), low),
            pltpu.VMEM((4, ROWS, half), low),
            pltpu.VMEM((4, ROWS, width), low),
            pltpu.VMEM((2, 2, ROWS, width), low),
            dma((4,)),
            dma((3,)),
            dma((2, 32)),
            dma((2, 3, 16)),
            dma((2, 5)),
            dma((2, 3)),
            dma((4, 2)),
            dma((4, 2)),
            dma((2, 4)),
            dma((2, 4)),
            dma((2, 4)),
            dma((2, 4)),
            dma((2,)),
            dma((4,)),
            dma((2,)),
            dma((2,)),
        ],
        compiler_params=pltpu.CompilerParams(
            collective_id=0, has_side_effects=True, vmem_limit_bytes=40 * 1024 * 1024
        ),
    )(*[pltpu.with_memory_space_constraint(a, pltpu.HBM) for a in operands])
    return pl.pallas_call(
        store_kernel,
        out_shape=outs,
        in_specs=[vmem] * 4,
        out_specs=(hbm,) * 4,
        scratch_shapes=[dma((13,))],
        compiler_params=pltpu.CompilerParams(vmem_limit_bytes=14 * 1024 * 1024),
    )(*results)


def is_slice_of_16(mesh):
    return mesh.shape["dp"] == 16 and mesh.shape["tensor"] == 2


def solution(mesh):
    per_device = per_device_fused if is_slice_of_16(mesh) else per_device_routed
    in_specs = (
        P(("dp", "tensor"), None),
        P(("dp", "tensor"), None),
        P(("dp", "tensor"), None),
        P(("dp", "tensor"), None),
        P("dp", None, "tensor"),
        P("dp", None, "tensor"),
        P("dp", "tensor", None),
    )
    out_specs = (
        P(("dp", "tensor"), None),
        P("dp", None, "tensor"),
        P("dp", None, "tensor"),
        P("dp", "tensor", None),
    )
    return jax.shard_map(
        per_device, mesh=mesh, in_specs=in_specs, out_specs=out_specs, check_vma=False
    )
```
